32 devices in a mesh: fsdp: 32 (over z, y, x, core).
Axes of the slice: x: 2, y: 2, z: 4, core: 2. Of those that a mesh axis runs over, the one named last changes fastest.
Arguments:
- tokens: bfloat16 [5760, 512], P('fsdp'), may hold values from -12 to 12
- cotangent: bfloat16 [5760, 512], P('fsdp'), may hold values from -6 to 6
- attention_in: bfloat16 [512, 2048], P('fsdp'), may hold values from -2 to 2
- attention_out: bfloat16 [512, 512], P('fsdp'), may hold values from -1 to 1
- first_in: bfloat16 [512, 2048], P('fsdp'), may hold values from -0.25 to 0.25
- first_out: bfloat16 [2048, 512], P(None, 'fsdp'), may hold values from -0.125 to 0.125
- second_in: bfloat16 [512, 2048], P('fsdp'), may hold values from -0.25 to 0.25
- second_out: bfloat16 [2048, 512], P(None, 'fsdp'), may hold values from -0.125 to 0.125
- pointwise_in: bfloat16 [512, 1024], P('fsdp'), may hold values from -0.25 to 0.25
- depthwise: bfloat16 [31, 512], P(None, 'fsdp'), may hold values from -1 to 1
- pointwise_out: bfloat16 [512, 512], P('fsdp'), may hold values from -0.25 to 0.25
- vectors: bfloat16 [14, 512], P(None, 'fsdp'), may hold values from -4 to 4
Outputs:
- output: bfloat16 [5760, 512], P('fsdp')
- grad_tokens: bfloat16 [5760, 512], P('fsdp')
- grad_attention_in: float32 [512, 2048], P('fsdp')
- grad_attention_out: float32 [512, 512], P('fsdp')
- grad_first_in: float32 [512, 2048], P('fsdp')
- grad_first_out: float32 [2048, 512], P(None, 'fsdp')
- grad_second_in: float32 [512, 2048], P('fsdp')
- grad_second_out: float32 [2048, 512], P(None, 'fsdp')
- grad_pointwise_in: float32 [512, 1024], P('fsdp')
- grad_depthwise: float32 [31, 512], P(None, 'fsdp')
- grad_pointwise_out: float32 [512, 512], P('fsdp')
- grad_vectors: float32 [14, 512], P(None, 'fsdp')
The draws below stay inside these ranges and needn't reach their ends.
All inputs are finite; a program needn't handle non-finite values.
Results may differ from the reference program's by a relative error of at most 0.03.
Values may be sent and summed in bfloat16 or wider, within the bound.
A program may use at most 192 MiB of HBM per device.

```python
import math
import jax
import jax.numpy as jnp
from jax import lax

D = 512
HEADS = 8
FF = 2048
HEAD = 64
KERNEL = 31
SEQ_LEN = 180
MICRO = 1
SEQS = 1
TOKENS = 5760
N_FSDP = 32


def draw_tokens(key, part):
    noise_key, direction_key = jax.random.split(key)
    count = TOKENS // SEQ_LEN
    order = (jnp.arange(TOKENS) // SEQ_LEN).astype(jnp.float32) / max(count - 1, 1)
    direction = jnp.clip(jax.random.normal(direction_key, (D,), jnp.float32), -4.0, 4.0)
    noise = jax.random.normal(noise_key, (TOKENS, D), jnp.float32)
    strength = 0.3 + 1.5 * order
    return jnp.clip(noise + strength[:, None] * direction[None, :], -12.0, 12.0).astype(jnp.bfloat16)


def draw_attention_in(key, part):
    base = jax.random.normal(key, (D, 4 * D), jnp.float32) / math.sqrt(D)
    return jnp.clip(base, -2.0, 2.0).astype(jnp.bfloat16)


def draw_vectors(key, part):
    noise = jax.random.normal(key, (14, D), jnp.float32)
    index = jnp.arange(14)[:, None]
    gains = jnp.logical_and(index % 2 == 0, index < 12)
    result = jnp.where(gains, 1.0 + 0.25 * noise, jnp.where(index < 12, 0.3 * noise, noise))
    return jnp.clip(result, -4.0, 4.0).astype(jnp.bfloat16)


def strengthened(array, stream_key, source, target, blocks, factor):
    def block_of(axis_at):
        return (jnp.arange(array.shape[axis_at]) // (array.shape[axis_at] // blocks)).reshape((-1,) + (1,) * (array.ndim - 1 - axis_at))

    one_side = jax.random.permutation(stream_key, blocks)[block_of(target)]
    second = (block_of(target) + blocks // 2) % blocks
    return jnp.where((block_of(source) == one_side) | (block_of(source) == second), factor * array, array)


def steps_of(stream_key, dims, shards, smallest, high):
    factor_of = 1.0
    for axis_at, parts in shards:
        heights = jax.random.uniform(jax.random.fold_in(jax.random.fold_in(stream_key, 6), axis_at), (parts,), jnp.float32, smallest / len(shards), high / len(shards))
        factor_of = factor_of * jnp.repeat(jnp.exp(heights), dims[axis_at] // parts).reshape((-1,) + (1,) * (len(dims) - 1 - axis_at))
    return factor_of


def gaussian(key, shape, scale, limit, cuts=(), held_as=jnp.bfloat16):
    entries = scale * jax.random.normal(key, shape, jnp.float32)
    if cuts:
        entries = entries * steps_of(key, shape, cuts, -0.22, 0.18)
    return jnp.clip(entries, -limit, limit).astype(held_as)


def gaussian_with(rng, shape, deviation, most, pieces, heavy, kind=jnp.bfloat16):
    values = deviation * jax.random.normal(rng, shape, jnp.float32)
    if pieces:
        values = values * steps_of(rng, shape, pieces, -0.22, 0.18)
    return jnp.clip(strengthened(values, jax.random.fold_in(rng, 3), *heavy), -most, most).astype(kind)


def setup_inputs(seed: int = 0) -> dict:
    key_list = jax.random.split(jax.random.key(seed), 13)
    tokens = draw_tokens(jax.random.fold_in(key_list[12], 71), 0)
    cotangent = gaussian_with(key_list[1], (TOKENS, D), 1.0, 6.0, ((0, 32),), (0, 1, 32, 2.75))
    attention_in = draw_attention_in(jax.random.fold_in(key_list[12], 71), 0)
    attention_out = gaussian(key_list[3], (D, D), (D // 16) ** -0.5, 1.0, ((0, 32),))
    first_in = gaussian(key_list[4], (D, FF), D ** -0.5, 0.25, ((0, 32),))
    first_out = gaussian(key_list[5], (FF, D), FF ** -0.5, 0.125, ((1, 32),))
    second_in = gaussian(key_list[6], (D, FF), D ** -0.5, 0.25, ((0, 32),))
    second_out = gaussian(key_list[7], (FF, D), FF ** -0.5, 0.125, ((1, 32),))
    pointwise_in = gaussian(key_list[8], (D, 2 * D), D ** -0.5, 0.25, ((0, 32),))
    depthwise = gaussian(key_list[9], (KERNEL, D), KERNEL ** -0.5, 1.0, ((1, 32),))
    pointwise_out = gaussian(key_list[10], (D, D), D ** -0.5, 0.25, ((0, 32),))
    vectors = draw_vectors(jax.random.fold_in(key_list[12], 71), 0)
    return dict(tokens=tokens, cotangent=cotangent, attention_in=attention_in, attention_out=attention_out, first_in=first_in, first_out=first_out, second_in=second_in, second_out=second_out, pointwise_in=pointwise_in, depthwise=depthwise, pointwise_out=pointwise_out, vectors=vectors)


EPS = 1e-05

def product(left, right):
    return jnp.dot(left, right, preferred_element_type=jnp.float32)

def product_left(left, right):
    return lax.dot_general(left, right, (((0,), (0,)), ((), ())), preferred_element_type=jnp.float32)

def product_right(left, right):
    return lax.dot_general(left, right, (((1,), (1,)), ((), ())), preferred_element_type=jnp.float32)

def contract(form, left, right):
    return jnp.einsum(form, left.astype(jnp.float32), right.astype(jnp.float32), precision=lax.Precision.HIGHEST)

def norm_forward(inputs, gain, shift):
    mean = lax.optimization_barrier(jnp.mean(inputs, -1, keepdims=True))
    centred = inputs - mean
    inverse = lax.rsqrt(lax.optimization_barrier(jnp.mean(centred * centred, -1, keepdims=True)) + EPS)
    scaled = centred * inverse
    return (scaled * gain + shift, scaled, inverse)

def norm_backward(grad, scaled, inverse, gain):
    inner = grad * gain
    result = inverse * (inner - lax.optimization_barrier(jnp.mean(inner, -1, keepdims=True)) - scaled * lax.optimization_barrier(jnp.mean(inner * scaled, -1, keepdims=True)))
    return (result, lax.optimization_barrier(jnp.sum(grad * scaled, 0)), lax.optimization_barrier(jnp.sum(grad, 0)))

def swish_slope(hidden):
    sigma = jax.nn.sigmoid(hidden)
    return sigma * (1.0 + hidden * (1.0 - sigma))

def position_table(length, width):
    count = 2 * length - 1
    distance = (length - 1 - jnp.arange(count)).astype(jnp.float32)[:, None]
    freqs = jnp.exp(-math.log(10000.0) * (2.0 * jnp.arange(width // 2).astype(jnp.float32)) / width)[None, :]
    angles = distance * freqs
    return jnp.concatenate([jnp.sin(angles), jnp.cos(angles)], 1).astype(jnp.bfloat16)

def skew(full):
    lead = full.shape[:-2]
    length = full.shape[-2]
    span = full.shape[-1]
    flipped = jnp.flip(full, -2).reshape(lead + (length * span,))
    flipped = jnp.concatenate([flipped, jnp.zeros(lead + (length,), full.dtype)], -1)
    return jnp.flip(flipped.reshape(lead + (length, span + 1))[..., :length], -2)

def unskew(grad):
    lead = grad.shape[:-2]
    length = grad.shape[-1]
    span = 2 * length - 1
    flipped = jnp.concatenate([jnp.flip(grad, -2), jnp.zeros(lead + (length, length), grad.dtype)], -1)
    flipped = flipped.reshape(lead + (2 * length * length,))[..., :length * span]
    return jnp.flip(flipped.reshape(lead + (length, span)), -2)

def attention_scores(query_u, query_v, keys, relative):
    content = contract('sihe,sjhe->shij', query_u, keys)
    position = contract('sihe,che->shic', query_v, relative)
    return (content + skew(position)) * HEAD ** (-0.5)

def attention_core(query_u, query_v, keys, values, relative):
    scores = attention_scores(query_u, query_v, keys, relative)
    top = lax.optimization_barrier(jnp.max(scores, -1, keepdims=True))
    logsum = top + jnp.log(lax.optimization_barrier(jnp.sum(jnp.exp(scores - top), -1, keepdims=True)))
    probs = jnp.exp(scores - logsum).astype(jnp.bfloat16)
    context = contract('shij,sjhe->sihe', probs, values)
    return (context.astype(jnp.bfloat16), logsum)

def attention_core_backward(query_u, query_v, keys, values, logsum, grad_context, relative):
    scores = attention_scores(query_u, query_v, keys, relative)
    probs = jnp.exp(scores - logsum)
    probs_low = probs.astype(jnp.bfloat16)
    grad_probs = contract('sihe,sjhe->shij', grad_context, values)
    grad_values = contract('shij,sihe->sjhe', probs_low, grad_context)
    delta = lax.optimization_barrier(jnp.sum(probs * grad_probs, -1, keepdims=True))
    grad_scores = (probs * (grad_probs - delta) * HEAD ** (-0.5)).astype(jnp.bfloat16)
    grad_u = contract('shij,sjhe->sihe', grad_scores, keys)
    grad_keys = contract('shij,sihe->sjhe', grad_scores, query_u)
    grad_full = unskew(grad_scores)
    grad_v = contract('shic,che->sihe', grad_full, relative)
    grad_relative = contract('shic,sihe->sche', grad_full, query_v).astype(jnp.bfloat16)
    return (grad_u, grad_v, grad_keys, grad_values, grad_relative)

def each_sequence(function, arrays):

    def single(items):
        results = function(*[item[None] for item in items])
        return tuple((result[0] for result in results))
    return lax.map(single, arrays)

def feed_forward(inputs, gain, shift, weight_up, weight_down):
    normed, scaled, inverse = norm_forward(inputs, gain, shift)
    normed_low = normed.astype(jnp.bfloat16)
    hidden = product(normed_low, weight_up)
    active = (hidden * jax.nn.sigmoid(hidden)).astype(jnp.bfloat16)
    return (inputs + 0.5 * product(active, weight_down), (normed_low, scaled, inverse, hidden, active))

def feed_backward(grad, saved, gain, weight_up, weight_down):
    normed_low, scaled, inverse, hidden, active = saved
    down_low = (0.5 * grad).astype(jnp.bfloat16)
    grad_down = product_left(active, down_low)
    grad_hidden = (product_right(down_low, weight_down) * swish_slope(hidden)).astype(jnp.bfloat16)
    grad_up = product_left(normed_low, grad_hidden)
    grad_input, grad_gain, grad_shift = norm_backward(product_right(grad_hidden, weight_up), scaled, inverse, gain)
    return (grad + grad_input, grad_up, grad_down, grad_gain, grad_shift)

def attention_layer(inputs, params, project_in, project_out, table, sequences, runner):
    width = inputs.shape[1]
    length = inputs.shape[0] // sequences
    normed, scaled, inverse = norm_forward(inputs, params[2], params[3])
    normed_low = normed.astype(jnp.bfloat16)
    joint = product(normed_low, project_in[:, :3 * width])
    query = joint[:, :width]
    shape = (sequences, length, HEADS, width // HEADS)
    keys = joint[:, width:2 * width].astype(jnp.bfloat16).reshape(shape)
    values = joint[:, 2 * width:].astype(jnp.bfloat16).reshape(shape)
    query_u = (query + params[12]).astype(jnp.bfloat16).reshape(shape)
    query_v = (query + params[13]).astype(jnp.bfloat16).reshape(shape)
    relative = product(table, project_in[:, 3 * width:]).astype(jnp.bfloat16).reshape(2 * length - 1, HEADS, width // HEADS)

    def attend(part_u, part_v, part_keys, part_values):
        return attention_core(part_u, part_v, part_keys, part_values, relative)
    context, logsum = runner(attend, (query_u, query_v, keys, values))
    context = context.reshape(-1, width)
    saved = (normed_low, scaled, inverse, query_u, query_v, keys, values, relative, logsum, context)
    return (inputs + product(context, project_out), saved)

def attention_layer_backward(grad, saved, params, project_in, project_out, table, sequences, runner):
    normed_low, scaled, inverse, query_u, query_v, keys, values, relative, logsum, context = saved
    width = grad.shape[1]
    grad_low = grad.astype(jnp.bfloat16)
    grad_out = product_left(context, grad_low)
    grad_context = product_right(grad_low, project_out).astype(jnp.bfloat16).reshape(query_u.shape)

    def attend_back(part_u, part_v, part_keys, part_values, part_logsum, part_grad):
        return attention_core_backward(part_u, part_v, part_keys, part_values, part_logsum, part_grad, relative)
    grad_u, grad_v, grad_keys, grad_values, grad_relative = runner(attend_back, (query_u, query_v, keys, values, logsum, grad_context))
    grad_joint = jnp.concatenate([(grad_u + grad_v).reshape(-1, width), grad_keys.reshape(-1, width), grad_values.reshape(-1, width)], 1).astype(jnp.bfloat16)
    grad_joint_in = product_left(normed_low, grad_joint)
    span = relative.shape[0]
    grad_position = product_left(jnp.tile(table, (sequences, 1)), grad_relative.reshape(sequences * span, width))
    grad_in = jnp.concatenate([grad_joint_in, grad_position], 1)
    grad_input, grad_gain, grad_shift = norm_backward(product_right(grad_joint, project_in[:, :3 * width]), scaled, inverse, params[2])
    return (grad + grad_input, grad_in, grad_out, grad_gain, grad_shift, lax.optimization_barrier(jnp.sum(grad_u, (0, 1))).reshape(width), lax.optimization_barrier(jnp.sum(grad_v, (0, 1))).reshape(width))

def mixer_head(inputs, gain, shift, weight_up, taps, sequences):
    normed, scaled, inverse = norm_forward(inputs, gain, shift)
    normed_low = normed.astype(jnp.bfloat16)
    joint = product(normed_low, weight_up)
    width = inputs.shape[1]
    sigma = jax.nn.sigmoid(joint[:, width:])
    gated = joint[:, :width] * sigma
    length = inputs.shape[0] // sequences
    half = (taps.shape[0] - 1) // 2
    padded = jnp.pad(gated.reshape(sequences, length, width), ((0, 0), (half, half), (0, 0)))
    depth = jnp.zeros((sequences, length, width), jnp.float32)
    for offset in range(taps.shape[0]):
        depth = depth + taps[offset] * padded[:, offset:offset + length]
    return (depth.reshape(-1, width), (normed_low, scaled, inverse, joint, sigma, padded))

def mixer_backward(grad, grad_depth, saved, taps, weight_up, gain, sequences):
    normed_low, scaled, inverse, joint, sigma, padded = saved
    width = grad.shape[1]
    length = grad.shape[0] // sequences
    kernel = taps.shape[0]
    half = (kernel - 1) // 2
    grad_cube = grad_depth.reshape(sequences, length, width)
    grad_padded = jnp.pad(grad_cube, ((0, 0), (half, half), (0, 0)))
    grad_gated = jnp.zeros((sequences, length, width), jnp.float32)
    tap_rows = []
    for offset in range(kernel):
        start = kernel - 1 - offset
        grad_gated = grad_gated + taps[offset] * grad_padded[:, start:start + length]
        tap_rows.append(lax.optimization_barrier(jnp.sum(grad_cube * padded[:, offset:offset + length], (0, 1))))
    grad_gated = grad_gated.reshape(-1, width)
    grad_joint = jnp.concatenate([grad_gated * sigma, grad_gated * joint[:, :width] * sigma * (1.0 - sigma)], 1).astype(jnp.bfloat16)
    grad_up = product_left(normed_low, grad_joint)
    grad_input, grad_gain, grad_shift = norm_backward(product_right(grad_joint, weight_up), scaled, inverse, gain)
    return (grad + grad_input, grad_up, jnp.stack(tap_rows), grad_gain, grad_shift)

def micro_step(rows, incoming, forward_set, backward_set, sequences, batch_stats, grad_stats, runner):
    project_in, project_out, first_up, first_down, second_up, second_down, mixer_up, mixer_taps, mixer_down, packed = forward_set
    params = packed.astype(jnp.float32)
    taps = mixer_taps.astype(jnp.float32)
    table = position_table(SEQ_LEN, rows.shape[1])
    inputs = rows.astype(jnp.float32)
    after_first, saved_first = feed_forward(inputs, params[0], params[1], first_up, first_down)
    after_attention, saved_attention = attention_layer(after_first, params, project_in, project_out, table, sequences, runner)
    depth, saved_mixer = mixer_head(after_attention, params[4], params[5], mixer_up, taps, sequences)
    batch_mean, batch_var = batch_stats(depth)
    inverse_var = lax.rsqrt(batch_var + EPS)
    batch_normal = (depth - batch_mean) * inverse_var
    batch_active = batch_normal * params[10] + params[11]
    mixer_active = (batch_active * jax.nn.sigmoid(batch_active)).astype(jnp.bfloat16)
    after_mixer = after_attention + product(mixer_active, mixer_down)
    after_second, saved_second = feed_forward(after_mixer, params[6], params[7], second_up, second_down)
    final, final_scaled, final_inverse = norm_forward(after_second, params[8], params[9])
    project_in, project_out, first_up, first_down, second_up, second_down, mixer_up, mixer_taps, mixer_down, packed = backward_set
    params = packed.astype(jnp.float32)
    taps = mixer_taps.astype(jnp.float32)
    grad_rows = incoming.astype(jnp.float32)
    grad_second, gain_final, shift_final = norm_backward(grad_rows, final_scaled, final_inverse, params[8])
    grad_mixer, grad_second_up, grad_second_down, gain_second, shift_second = feed_backward(grad_second, saved_second, params[6], second_up, second_down)
    mixer_low = grad_mixer.astype(jnp.bfloat16)
    grad_mixer_down = product_left(mixer_active, mixer_low)
    grad_batch = product_right(mixer_low, mixer_down) * swish_slope(batch_active)
    mean_grad, mean_cross = grad_stats(grad_batch, batch_normal)
    grad_depth = params[10] * inverse_var * (grad_batch - mean_grad - batch_normal * mean_cross)
    grad_attention, grad_mixer_up, grad_taps, gain_mixer, shift_mixer = mixer_backward(grad_mixer, grad_depth, saved_mixer, taps, mixer_up, params[4], sequences)
    grad_first, grad_project_in, grad_project_out, gain_attention, shift_attention, grad_bias_u, grad_bias_v = attention_layer_backward(grad_attention, saved_attention, params, project_in, project_out, table, sequences, runner)
    grad_inputs, grad_first_up, grad_first_down, gain_first, shift_first = feed_backward(grad_first, saved_first, params[0], first_up, first_down)
    grad_packed = jnp.stack([gain_first, shift_first, gain_attention, shift_attention, gain_mixer, shift_mixer, gain_second, shift_second, gain_final, shift_final, lax.optimization_barrier(jnp.sum(grad_batch * batch_normal, 0)), lax.optimization_barrier(jnp.sum(grad_batch, 0)), grad_bias_u, grad_bias_v])
    grads = (grad_project_in, grad_project_out, grad_first_up, grad_first_down, grad_second_up, grad_second_down, grad_mixer_up, grad_taps, grad_mixer_down, grad_packed)
    return (final.astype(jnp.bfloat16), grad_inputs.astype(jnp.bfloat16), grads)

def batch_stats(depth):
    mean = lax.optimization_barrier(jnp.mean(depth, 0))
    centred = depth - mean
    return (mean, lax.optimization_barrier(jnp.mean(centred * centred, 0)))

def grad_stats(grad_batch, batch_normal):
    return (lax.optimization_barrier(jnp.mean(grad_batch, 0)), lax.optimization_barrier(jnp.mean(grad_batch * batch_normal, 0)))

def reference(tokens, cotangent, attention_in, attention_out, first_in, first_out, second_in, second_out, pointwise_in, depthwise, pointwise_out, vectors):
    block = SEQS * SEQ_LEN
    weights = (attention_in, attention_out, first_in, first_out, second_in, second_out, pointwise_in, depthwise, pointwise_out, vectors)
    inputs_all = tokens.reshape(N_FSDP, MICRO, block, D)
    grads_all = cotangent.reshape(N_FSDP, MICRO, block, D)
    outputs = []
    input_grads = []
    totals = ()
    for micro in range(MICRO):
        rows = inputs_all[:, micro].reshape(N_FSDP * block, D)
        incoming = grads_all[:, micro].reshape(N_FSDP * block, D)
        result, grad_rows, grads = micro_step(rows, incoming, weights, weights, N_FSDP * SEQS, batch_stats, grad_stats, each_sequence)
        outputs.append(result.reshape(N_FSDP, 1, block, D))
        input_grads.append(grad_rows.reshape(N_FSDP, 1, block, D))
        totals = grads if micro == 0 else tuple((left + right for left, right in zip(totals, grads)))
    output = jnp.concatenate(outputs, 1).reshape(TOKENS, D)
    grad_tokens = jnp.concatenate(input_grads, 1).reshape(TOKENS, D)
    return (output, grad_tokens, totals[0], totals[1], totals[2], totals[3], totals[4], totals[5], totals[6], totals[7], totals[8], totals[9])
```

```python
import functools
import math

import jax
import jax.numpy as jnp
from jax import lax
from jax.experimental import pallas as pl
from jax.experimental.pallas import tpu as pltpu
from jax.sharding import PartitionSpec as P

HEADS = 8
HEAD = 64
SEQ_LEN = 180
MICRO = 1


EPS = 1e-05


def exchange(block, axis, bit):
    count = lax.axis_size(axis)
    return lax.ppermute(block, axis, [(low, low ^ 1 << bit) for low in range(count)])


def bit_orders(levels):
    rest = list(range(1, levels))
    if levels == 5:
        return ((0, 1, 2, 3, 4), (0, 2, 1, 3, 4), (0, 3, 4, 1, 2))
    third = max(1, len(rest) // 3)
    return tuple(tuple([0] + rest[k:] + rest[:k]) for k in (0, third, 2 * third))


def gather_rows(shard, axis, order):
    me = lax.axis_index(axis)
    current = shard
    have = []
    for bit in reversed(order):
        other = exchange(current, axis, bit)
        have = sorted(have + [bit], reverse=True)
        low = jnp.right_shift(me, bit) % 2 == 0
        current = jnp.stack(
            [jnp.where(low, current, other), jnp.where(low, other, current)], have.index(bit)
        )
    return current.reshape(-1, shard.shape[1])


def scatter_rows(block, axis, order):
    count = lax.axis_size(axis)
    me = lax.axis_index(axis)
    current = block.reshape((2,) * len(order) + (block.shape[0] // count, block.shape[1]))
    left = sorted(order, reverse=True)
    for step, bit in enumerate(order):
        place = left.index(bit)
        left.remove(bit)
        mine = jnp.right_shift(me, bit) % 2
        keep = lax.dynamic_index_in_dim(current, mine, place, False)
        send = lax.dynamic_index_in_dim(current, 1 - mine, place, False)
        current = keep.astype(jnp.float32) + exchange(send, axis, bit).astype(jnp.float32)
        if step + 1 < len(order):
            current = current.astype(jnp.bfloat16)
    return current


def combine_kernel(levels, merge, in_ref, out_ref, slots, send_sems, recv_sems):
    me = lax.axis_index("fsdp")
    partners = []
    for bit in range(levels):
        step = 1 << bit
        partners.append(me + step - 2 * step * ((me // step) % 2))
    barrier = pltpu.get_barrier_semaphore()
    for partner in partners:
        pl.semaphore_signal(
            barrier, inc=1, device_id=(partner,), device_id_type=pl.DeviceIdType.MESH
        )
    pl.semaphore_wait(barrier, levels)
    slots[0] = in_ref[...]
    for bit in range(levels):
        copy = pltpu.make_async_remote_copy(
            src_ref=slots.at[2 * bit],
            dst_ref=slots.at[2 * bit + 1],
            send_sem=send_sems.at[bit],
            recv_sem=recv_sems.at[bit],
            device_id=(partners[bit],),
            device_id_type=pl.DeviceIdType.MESH,
        )
        copy.start()
        copy.wait()
        slots[2 * bit + 2] = merge(slots[2 * bit], slots[2 * bit + 1], 1 << bit)
    out_ref[...] = slots[2 * levels]


def combine(rows, merge, name, collective_id):
    levels = lax.axis_size("fsdp").bit_length() - 1
    return pl.pallas_call(
        functools.partial(combine_kernel, levels, merge),
        out_shape=jax.ShapeDtypeStruct(rows.shape, rows.dtype),
        in_specs=[pl.BlockSpec(memory_space=pltpu.VMEM)],
        out_specs=pl.BlockSpec(memory_space=pltpu.VMEM),
        scratch_shapes=[
            pltpu.VMEM((2 * levels + 1,) + rows.shape, rows.dtype),
            pltpu.SemaphoreType.DMA((levels,)),
            pltpu.SemaphoreType.DMA((levels,)),
        ],
        compiler_params=pltpu.CompilerParams(collective_id=collective_id, has_side_effects=True),
        name=name,
    )(rows)


def merge_sums(left, right, blocks):
    return left + right


def product(left, right):
    return jnp.dot(left, right, preferred_element_type=jnp.float32)


def product_left(left, right):
    return lax.dot_general(
        left, right, (((0,), (0,)), ((), ())), preferred_element_type=jnp.float32
    )


def product_right(left, right):
    return lax.dot_general(
        left, right, (((1,), (1,)), ((), ())), preferred_element_type=jnp.float32
    )


def contract(form, left, right):
    return jnp.einsum(form, left, right, preferred_element_type=jnp.float32)


def norm_forward(inputs, gain, shift):
    mean = jnp.mean(inputs, -1, keepdims=True)
    centred = inputs - mean
    inverse = lax.rsqrt(jnp.mean(centred * centred, -1, keepdims=True) + EPS)
    scaled = centred * inverse
    return (scaled * gain + shift, scaled, inverse)


def norm_backward(grad, scaled, inverse, gain):
    inner = grad * gain
    result = inverse * (
        inner
        - jnp.mean(inner, -1, keepdims=True)
        - scaled * jnp.mean(inner * scaled, -1, keepdims=True)
    )
    return (result, jnp.sum(grad * scaled, 0), jnp.sum(grad, 0))


def swish_slope(hidden):
    sigma = jax.nn.sigmoid(hidden)
    return sigma * (1.0 + hidden * (1.0 - sigma))


def position_table(length, width):
    count = 2 * length - 1
    distance = (length - 1 - jnp.arange(count)).astype(jnp.float32)[:, None]
    freqs = jnp.exp(
        -math.log(10000.0) * (2.0 * jnp.arange(width // 2).astype(jnp.float32)) / width
    )[None, :]
    angles = distance * freqs
    return jnp.concatenate([jnp.sin(angles), jnp.cos(angles)], 1).astype(jnp.bfloat16)


def skew(full):
    lead = full.shape[:-2]
    length = full.shape[-2]
    span = full.shape[-1]
    flat = full.reshape(lead + (length * span,))[..., length - 1 :]
    flat = flat[..., : length * (span - 1)]
    return flat.reshape(lead + (length, span - 1))[..., :length]


def unskew(grad):
    lead = grad.shape[:-2]
    length = grad.shape[-1]
    span = 2 * length - 1
    none = [(0, 0)] * len(lead)
    flat = jnp.pad(grad, none + [(0, 0), (0, span - 1 - length)])
    flat = flat.reshape(lead + (length * (span - 1),))
    flat = jnp.pad(flat, none + [(length - 1, 1)])
    return flat.reshape(lead + (length, span))


def attention_scores(query_u, query_v, keys, relative):
    content = contract("sihe,sjhe->shij", query_u, keys)
    position = contract("sihe,che->shic", query_v, relative)
    return (content + skew(position)) * HEAD ** (-0.5)


def attention_core(query_u, query_v, keys, values, relative):
    scores = attention_scores(query_u, query_v, keys, relative)
    top = jnp.max(scores, -1, keepdims=True)
    logsum = top + jnp.log(jnp.sum(jnp.exp(scores - top), -1, keepdims=True))
    probs = jnp.exp(scores - logsum).astype(jnp.bfloat16)
    context = contract("shij,sjhe->sihe", probs, values)
    return (context.astype(jnp.bfloat16), logsum)


def attention_core_backward(query_u, query_v, keys, values, logsum, grad_context, relative):
    scores = attention_scores(query_u, query_v, keys, relative)
    probs = jnp.exp(scores - logsum)
    probs_low = probs.astype(jnp.bfloat16)
    grad_probs = contract("sihe,sjhe->shij", grad_context, values)
    grad_values = contract("shij,sihe->sjhe", probs_low, grad_context)
    delta = jnp.sum(probs * grad_probs, -1, keepdims=True)
    grad_scores = (probs * (grad_probs - delta) * HEAD ** (-0.5)).astype(jnp.bfloat16)
    grad_u = contract("shij,sjhe->sihe", grad_scores, keys)
    grad_keys = contract("shij,sihe->sjhe", grad_scores, query_u)
    grad_full = unskew(grad_scores)
    grad_v = contract("shic,che->sihe", grad_full, relative)
    grad_relative = contract("shic,sihe->sche", grad_full, query_v).astype(jnp.bfloat16)
    return (grad_u, grad_v, grad_keys, grad_values, grad_relative)


def all_at_once(function, arrays):
    return function(*arrays)


def feed_forward(inputs, gain, shift, weight_up, weight_down):
    normed, scaled, inverse = norm_forward(inputs, gain, shift)
    normed_low = normed.astype(jnp.bfloat16)
    hidden = product(normed_low, weight_up)
    active = (hidden * jax.nn.sigmoid(hidden)).astype(jnp.bfloat16)
    return (
        inputs + 0.5 * product_right(active, weight_down),
        (normed_low, scaled, inverse, hidden, active),
    )


def feed_backward(grad, saved, gain, weight_up, weight_down):
    normed_low, scaled, inverse, hidden, active = saved
    down_low = (0.5 * grad).astype(jnp.bfloat16)
    grad_down = product_left(down_low, active)
    grad_hidden = (product(down_low, weight_down) * swish_slope(hidden)).astype(jnp.bfloat16)
    grad_up = product_left(normed_low, grad_hidden)
    grad_input, grad_gain, grad_shift = norm_backward(
        product_right(grad_hidden, weight_up), scaled, inverse, gain
    )
    return (grad + grad_input, grad_up, grad_down, grad_gain, grad_shift)


def attention_layer(inputs, params, project_in, project_out, table, sequences, runner):
    width = inputs.shape[1]
    length = inputs.shape[0] // sequences
    normed, scaled, inverse = norm_forward(inputs, params[2], params[3])
    normed_low = normed.astype(jnp.bfloat16)
    joint = product(normed_low, project_in[:, : 3 * width])
    query = joint[:, :width]
    shape = (sequences, length, HEADS, width // HEADS)
    keys = joint[:, width : 2 * width].astype(jnp.bfloat16).reshape(shape)
    values = joint[:, 2 * width :].astype(jnp.bfloat16).reshape(shape)
    query_u = (query + params[12]).astype(jnp.bfloat16).reshape(shape)
    query_v = (query + params[13]).astype(jnp.bfloat16).reshape(shape)
    relative = (
        product(table, project_in[:, 3 * width :])
        .astype(jnp.bfloat16)
        .reshape(2 * length - 1, HEADS, width // HEADS)
    )

    def attend(part_u, part_v, part_keys, part_values):
        return attention_core(part_u, part_v, part_keys, part_values, relative)

    context, logsum = runner(attend, (query_u, query_v, keys, values))
    context = context.reshape(-1, width)
    saved = (normed_low, scaled, inverse, query_u, query_v, keys, values, relative, logsum, context)
    return (inputs + product(context, project_out), saved)


def attention_layer_backward(
    grad, saved, params, project_in, project_out, table, sequences, runner
):
    normed_low, scaled, inverse, query_u, query_v, keys, values, relative, logsum, context = saved
    width = grad.shape[1]
    grad_low = grad.astype(jnp.bfloat16)
    grad_out = product_left(context, grad_low)
    grad_context = product_right(grad_low, project_out).astype(jnp.bfloat16).reshape(query_u.shape)

    def attend_back(part_u, part_v, part_keys, part_values, part_logsum, part_grad):
        return attention_core_backward(
            part_u, part_v, part_keys, part_values, part_logsum, part_grad, relative
        )

    grad_u, grad_v, grad_keys, grad_values, grad_relative = runner(
        attend_back, (query_u, query_v, keys, values, logsum, grad_context)
    )
    grad_joint = jnp.concatenate(
        [
            (grad_u + grad_v).reshape(-1, width),
            grad_keys.reshape(-1, width),
            grad_values.reshape(-1, width),
        ],
        1,
    ).astype(jnp.bfloat16)
    grad_joint_in = product_left(normed_low, grad_joint)
    span = relative.shape[0]
    grad_position = product_left(
        jnp.tile(table, (sequences, 1)), grad_relative.reshape(sequences * span, width)
    )
    grad_in = jnp.concatenate([grad_joint_in, grad_position], 1)
    grad_input, grad_gain, grad_shift = norm_backward(
        product_right(grad_joint, project_in[:, : 3 * width]), scaled, inverse, params[2]
    )
    return (
        grad + grad_input,
        grad_in,
        grad_out,
        grad_gain,
        grad_shift,
        jnp.sum(grad_u, (0, 1)).reshape(width),
        jnp.sum(grad_v, (0, 1)).reshape(width),
    )


def mixer_head(inputs, gain, shift, weight_up, taps, sequences):
    normed, scaled, inverse = norm_forward(inputs, gain, shift)
    normed_low = normed.astype(jnp.bfloat16)
    joint = product(normed_low, weight_up)
    width = inputs.shape[1]
    sigma = jax.nn.sigmoid(joint[:, width:])
    gated = joint[:, :width] * sigma
    length = inputs.shape[0] // sequences
    half = (taps.shape[0] - 1) // 2
    padded = jnp.pad(gated.reshape(sequences, length, width), ((0, 0), (half, half), (0, 0)))
    depth = jnp.zeros((sequences, length, width), jnp.float32)
    for offset in range(taps.shape[0]):
        depth = depth + taps[offset] * padded[:, offset : offset + length]
    return (depth.reshape(-1, width), (normed_low, scaled, inverse, joint, sigma, padded))


def mixer_backward(grad, grad_depth, saved, taps, weight_up, gain, sequences):
    normed_low, scaled, inverse, joint, sigma, padded = saved
    width = grad.shape[1]
    length = grad.shape[0] // sequences
    kernel = taps.shape[0]
    half = (kernel - 1) // 2
    grad_cube = grad_depth.reshape(sequences, length, width)
    grad_padded = jnp.pad(grad_cube, ((0, 0), (half, half), (0, 0)))
    grad_gated = jnp.zeros((sequences, length, width), jnp.float32)
    tap_rows = []
    for offset in range(kernel):
        start = kernel - 1 - offset
        grad_gated = grad_gated + taps[offset] * grad_padded[:, start : start + length]
        tap_rows.append(jnp.sum(grad_cube * padded[:, offset : offset + length], (0, 1)))
    grad_gated = grad_gated.reshape(-1, width)
    grad_joint = jnp.concatenate(
        [grad_gated * sigma, grad_gated * joint[:, :width] * sigma * (1.0 - sigma)], 1
    ).astype(jnp.bfloat16)
    grad_up = product_left(normed_low, grad_joint)
    grad_input, grad_gain, grad_shift = norm_backward(
        product_right(grad_joint, weight_up), scaled, inverse, gain
    )
    return (grad + grad_input, grad_up, jnp.stack(tap_rows), grad_gain, grad_shift)


def micro_step(
    rows, incoming, forward_set, backward_set, sequences, batch_stats, grad_stats, runner
):
    (
        project_in,
        project_out,
        first_up,
        first_down,
        second_up,
        second_down,
        mixer_up,
        mixer_taps,
        mixer_down,
        packed,
    ) = forward_set
    params = packed.astype(jnp.float32)
    taps = mixer_taps.astype(jnp.float32)
    table = position_table(SEQ_LEN, rows.shape[1])
    inputs = rows.astype(jnp.float32)
    after_first, saved_first = feed_forward(inputs, params[0], params[1], first_up, first_down)
    after_attention, saved_attention = attention_layer(
        after_first, params, project_in, project_out, table, sequences, runner
    )
    depth, saved_mixer = mixer_head(
        after_attention, params[4], params[5], mixer_up, taps, sequences
    )
    batch_mean, batch_var = batch_stats(depth)
    inverse_var = lax.rsqrt(batch_var + EPS)
    batch_normal = (depth - batch_mean) * inverse_var
    batch_active = batch_normal * params[10] + params[11]
    mixer_active = (batch_active * jax.nn.sigmoid(batch_active)).astype(jnp.bfloat16)
    after_mixer = after_attention + product(mixer_active, mixer_down)
    after_second, saved_second = feed_forward(
        after_mixer, params[6], params[7], second_up, second_down
    )
    final, final_scaled, final_inverse = norm_forward(after_second, params[8], params[9])
    (
        project_in,
        project_out,
        first_up,
        first_down,
        second_up,
        second_down,
        mixer_up,
        mixer_taps,
        mixer_down,
        packed,
    ) = backward_set
    params = packed.astype(jnp.float32)
    taps = mixer_taps.astype(jnp.float32)
    grad_rows = incoming.astype(jnp.float32)
    grad_second, gain_final, shift_final = norm_backward(
        grad_rows, final_scaled, final_inverse, params[8]
    )
    grad_mixer, grad_second_up, grad_second_down, gain_second, shift_second = feed_backward(
        grad_second, saved_second, params[6], second_up, second_down
    )
    mixer_low = grad_mixer.astype(jnp.bfloat16)
    grad_mixer_down = product_left(mixer_active, mixer_low)
    grad_batch = product_right(mixer_low, mixer_down) * swish_slope(batch_active)
    mean_grad, mean_cross = grad_stats(grad_batch, batch_normal)
    grad_depth = params[10] * inverse_var * (grad_batch - mean_grad - batch_normal * mean_cross)
    grad_attention, grad_mixer_up, grad_taps, gain_mixer, shift_mixer = mixer_backward(
        grad_mixer, grad_depth, saved_mixer, taps, mixer_up, params[4], sequences
    )
    (
        grad_first,
        grad_project_in,
        grad_project_out,
        gain_attention,
        shift_attention,
        grad_bias_u,
        grad_bias_v,
    ) = attention_layer_backward(
        grad_attention, saved_attention, params, project_in, project_out, table, sequences, runner
    )
    grad_inputs, grad_first_up, grad_first_down, gain_first, shift_first = feed_backward(
        grad_first, saved_first, params[0], first_up, first_down
    )
    grad_packed = jnp.stack(
        [
            gain_first,
            shift_first,
            gain_attention,
            shift_attention,
            gain_mixer,
            shift_mixer,
            gain_second,
            shift_second,
            gain_final,
            shift_final,
            jnp.sum(grad_batch * batch_normal, 0),
            jnp.sum(grad_batch, 0),
            grad_bias_u,
            grad_bias_v,
        ]
    )
    grads = (
        grad_project_in,
        grad_project_out,
        grad_first_up,
        grad_first_down,
        grad_second_up,
        grad_second_down,
        grad_mixer_up,
        grad_taps,
        grad_mixer_down,
        grad_packed,
    )
    return (final.astype(jnp.bfloat16), grad_inputs.astype(jnp.bfloat16), grads)


def on_device(
    tokens,
    cotangent,
    attention_in,
    attention_out,
    first_in,
    first_out,
    second_in,
    second_out,
    pointwise_in,
    depthwise,
    pointwise_out,
    vectors,
):
    block = tokens.shape[0] // MICRO
    sequences = block // SEQ_LEN
    owners = lax.axis_size("fsdp")
    count = block * owners

    def merge_moments(left, right, blocks):
        gap = left[0:1] - right[0:1]
        mean = 0.5 * (left[0:1] + right[0:1])
        squares = left[1:2] + right[1:2] + (0.5 * blocks * block) * gap * gap
        return jnp.concatenate([mean, squares], 0)

    def batch_stats(depth):
        mean = jnp.mean(depth, 0, keepdims=True)
        centred = depth - mean
        moments = jnp.concatenate([mean, jnp.sum(centred * centred, 0, keepdims=True)], 0)
        moments = combine(moments, merge_moments, "moments", 0)
        return (moments[0], moments[1] / count)

    def grad_stats(grad_batch, batch_normal):
        sums = jnp.stack([jnp.sum(grad_batch, 0), jnp.sum(grad_batch * batch_normal, 0)])
        sums = combine(sums, merge_sums, "sums", 1)
        return (sums[0] / count, sums[1] / count)

    orders = bit_orders(owners.bit_length() - 1)
    small = jnp.concatenate([depthwise, vectors], 0)
    small = jnp.pad(small.T, ((0, 0), (0, 128 - small.shape[0])))
    first = gather_rows(jnp.concatenate([first_in, first_out.T, small], 1), "fsdp", orders[0])
    middle = gather_rows(
        jnp.concatenate([attention_in, attention_out, pointwise_in, pointwise_out], 1),
        "fsdp",
        orders[1],
    )
    second = gather_rows(jnp.concatenate([second_in, second_out.T], 1), "fsdp", orders[2])
    width = first_out.shape[0]
    packed = first[:, 2 * width :].T
    taps = depthwise.shape[0]
    cuts = [attention_in.shape[1]]
    for part in (attention_out, pointwise_in):
        cuts.append(cuts[-1] + part.shape[1])
    shared = (
        middle[:, : cuts[0]],
        middle[:, cuts[0] : cuts[1]],
        first[:, :width],
        first[:, width : 2 * width],
        second[:, :width],
        second[:, width:],
        middle[:, cuts[1] : cuts[2]],
        packed[:taps],
        middle[:, cuts[2] :],
        packed[taps : taps + vectors.shape[0]],
    )
    result, grad_rows, grads = micro_step(
        tokens, cotangent, shared, shared, sequences, batch_stats, grad_stats, all_at_once
    )
    low = [grad.astype(jnp.bfloat16) for grad in grads]
    small = jnp.concatenate([low[7], low[9]], 0)
    small = jnp.pad(small.T, ((0, 0), (0, 128 - small.shape[0])))
    second = scatter_rows(jnp.concatenate([low[4], low[5]], 1), "fsdp", orders[2])
    middle = scatter_rows(
        jnp.concatenate([low[0], low[1], low[6], low[8]], 1), "fsdp", orders[1]
    )
    first = scatter_rows(jnp.concatenate([low[2], low[3], small], 1), "fsdp", orders[0])
    packed = first[:, 2 * width :].T
    return (
        result,
        grad_rows,
        middle[:, : cuts[0]],
        middle[:, cuts[0] : cuts[1]],
        first[:, :width],
        first[:, width : 2 * width].T,
        second[:, :width],
        second[:, width:].T,
        middle[:, cuts[1] : cuts[2]],
        packed[:taps],
        middle[:, cuts[2] :],
        packed[taps : taps + vectors.shape[0]],
    )


def solution(mesh):
    return jax.shard_map(
        on_device,
        mesh=mesh,
        in_specs=(
            P("fsdp", None),
            P("fsdp", None),
            P("fsdp", None),
            P("fsdp", None),
            P("fsdp", None),
            P(None, "fsdp"),
            P("fsdp", None),
            P(None, "fsdp"),
            P("fsdp", None),
            P(None, "fsdp"),
            P("fsdp", None),
            P(None, "fsdp"),
        ),
        out_specs=(
            P("fsdp", None),
            P("fsdp", None),
            P("fsdp", None),
            P("fsdp", None),
            P("fsdp", None),
            P(None, "fsdp"),
            P("fsdp", None),
            P(None, "fsdp"),
            P("fsdp", None),
            P(None, "fsdp"),
            P("fsdp", None),
            P(None, "fsdp"),
        ),
        check_vma=False,
    )
```

```python
import functools
import math

import jax
import jax.numpy as jnp
from jax import lax
from jax.experimental import pallas as pl
from jax.experimental.pallas import tpu as pltpu
from jax.sharding import PartitionSpec as P

HEADS = 8
HEAD = 64
SEQ_LEN = 180
MICRO = 1


EPS = 1e-05


def exchange(block, axis, bit):
    count = lax.axis_size(axis)
    return lax.ppermute(block, axis, [(low, low ^ 1 << bit) for low in range(count)])


def bit_orders(levels):
    rest = list(range(1, levels))
    if levels == 5:
        return ((0, 1, 2, 3, 4), (0, 2, 1, 3, 4), (0, 3, 4, 1, 2))
    third = max(1, len(rest) // 3)
    return tuple(tuple([0] + rest[k:] + rest[:k]) for k in (0, third, 2 * third))


def gather_rows(shard, axis, order):
    me = lax.axis_index(axis)
    current = shard
    have = []
    for bit in reversed(order):
        other = exchange(current, axis, bit)
        have = sorted(have + [bit], reverse=True)
        low = jnp.right_shift(me, bit) % 2 == 0
        current = jnp.stack(
            [jnp.where(low, current, other), jnp.where(low, other, current)], have.index(bit)
        )
    return current.reshape(-1, shard.shape[1])


def scatter_rows(block, axis, order):
    return scatter_turns(split_rows(block, axis), axis, order, 0, len(order))


def split_rows(block, axis):
    count = lax.axis_size(axis)
    return block.reshape(
        (2,) * (count.bit_length() - 1) + (block.shape[0] // count, block.shape[1])
    )


def scatter_turns(current, axis, order, begin, end):
    me = lax.axis_index(axis)
    left = sorted(order[begin:], reverse=True)
    for step, bit in list(enumerate(order))[begin:end]:
        place = left.index(bit)
        left.remove(bit)
        mine = jnp.right_shift(me, bit) % 2
        keep = lax.dynamic_index_in_dim(current, mine, place, False)
        send = lax.dynamic_index_in_dim(current, 1 - mine, place, False)
        current = keep.astype(jnp.float32) + exchange(send, axis, bit).astype(jnp.float32)
        if step + 1 < len(order):
            current = current.astype(jnp.bfloat16)
    return current


def partner_of(me, bit):
    step = 1 << bit
    return me + step - 2 * step * ((me // step) % 2)


def column_runs(width):
    large = width * 7 // 16 // 128 * 128
    return ((0, large), (large, large), (2 * large, width - 2 * large))


def gather_kernel(orders, count, *refs):
    levels = len(orders[0])
    shards = refs[:count]
    wholes = refs[count : 2 * count]
    local_sems, send_sems, recv_sems = refs[2 * count :]
    me = lax.axis_index("fsdp")
    partners = [partner_of(me, bit) for bit in range(levels)]
    barrier = pltpu.get_barrier_semaphore()
    for partner in partners:
        pl.semaphore_signal(
            barrier, inc=1, device_id=(partner,), device_id_type=pl.DeviceIdType.MESH
        )
    pl.semaphore_wait(barrier, levels)

    def held(done):
        return tuple(
            slice(None) if bit in done else (me // (1 << bit)) % 2
            for bit in reversed(range(levels))
        )

    own = []
    for index in range(count):
        own.append(
            pltpu.make_async_copy(
                shards[index], wholes[index].at[held(())], local_sems.at[index]
            )
        )
        own[-1].start()
    flying = {}
    for step in range(levels + count - 1):
        for index in range(count):
            turn = step - index
            if turn < 0 or turn >= levels:
                continue
            width = shards[index].shape[1]
            for lane, order in enumerate(orders):
                start, size = column_runs(width)[lane]
                chain = index * len(orders) + lane
                route = order[::-1]
                if turn > 0:
                    flying[chain].wait()
                    if turn == 1 and lane == 0:
                        own[index].wait()
                columns = pl.ds(start, size)
                slot = wholes[index].at[held(route[:turn]) + (slice(None), columns)]
                source = shards[index].at[:, columns] if turn == 0 else slot
                flying[chain] = pltpu.make_async_remote_copy(
                    src_ref=source,
                    dst_ref=slot,
                    send_sem=send_sems.at[chain, turn],
                    recv_sem=recv_sems.at[chain, turn],
                    device_id=(partners[route[turn]],),
                    device_id_type=pl.DeviceIdType.MESH,
                )
                flying[chain].start()
    for copy in flying.values():
        copy.wait()


def gather_all(shards, orders):
    if shards[0].shape[0] % 16:
        return [gather_rows(shard, "fsdp", order) for shard, order in zip(shards, orders)]
    levels = len(orders[0])
    count = len(shards)
    wholes = pl.pallas_call(
        functools.partial(gather_kernel, orders, count),
        out_shape=[
            jax.ShapeDtypeStruct((2,) * levels + shard.shape, shard.dtype) for shard in shards
        ],
        in_specs=[pl.BlockSpec(memory_space=pl.ANY)] * count,
        out_specs=[pl.BlockSpec(memory_space=pl.ANY)] * count,
        scratch_shapes=[
            pltpu.SemaphoreType.DMA((count,)),
            pltpu.SemaphoreType.DMA((count * len(orders), levels)),
            pltpu.SemaphoreType.DMA((count * len(orders), levels)),
        ],
        compiler_params=pltpu.CompilerParams(collective_id=2, has_side_effects=True),
        name="gather",
    )(*shards)
    return [whole.reshape(-1, whole.shape[-1]) for whole in wholes]


def scatter_kernel(orders, count, *refs):
    levels = len(orders[0])
    grads = refs[:count]
    sums = refs[count : 2 * count]
    chains = count * len(orders)
    slots = refs[2 * count : -2]
    send_sems, recv_sems = refs[-2:]
    me = lax.axis_index("fsdp")
    partners = [partner_of(me, bit) for bit in range(levels)]
    mine = [(me // (1 << bit)) % 2 for bit in range(levels)]
    barrier = pltpu.get_barrier_semaphore()
    for partner in partners:
        pl.semaphore_signal(
            barrier, inc=1, device_id=(partner,), device_id_type=pl.DeviceIdType.MESH
        )
    pl.semaphore_wait(barrier, levels)

    def place_of(order, turn):
        left = sorted(order[turn:], reverse=True)
        return left.index(order[turn])

    def add(index, lane, turn):
        order = orders[lane]
        start, size = column_runs(grads[index].shape[-1])[lane]
        chain = index * len(orders) + lane
        columns = pl.ds(start, size)
        place = place_of(order, turn)
        depth = levels - 1 - turn
        arrived = slots[chain * levels + turn]
        before = slots[chain * levels + turn - 1]

        def body(block, carry):
            where = [(block // (1 << k)) % 2 for k in reversed(range(depth))]
            inner = tuple(where[:place] + [mine[order[turn]]] + where[place:])
            rows = (slice(None), slice(None))
            if turn == 0:
                kept = grads[index][inner + (slice(None), columns)]
            else:
                kept = before[inner + rows]
            total = kept.astype(jnp.float32) + arrived[tuple(where) + rows].astype(jnp.float32)
            if depth == 0:
                sums[index][:, columns] = total
            else:
                arrived[tuple(where) + rows] = total.astype(arrived.dtype)
            return carry

        if depth == 0:
            body(0, 0)
        else:
            lax.fori_loop(0, 1 << depth, body, 0)

    flying = {}
    for step in range(levels + count):
        for index in range(count):
            turn = step - index
            if turn < 0 or turn > levels:
                continue
            for lane, order in enumerate(orders):
                start, size = column_runs(grads[index].shape[-1])[lane]
                chain = index * len(orders) + lane
                if turn > 0:
                    flying[chain].wait()
                    add(index, lane, turn - 1)
                if turn == levels:
                    continue
                place = place_of(order, turn)
                away = (slice(None),) * place + (1 - mine[order[turn]],)
                away = away + (slice(None),) * (levels - 1 - turn - place)
                if turn == 0:
                    source = grads[index].at[away + (slice(None), pl.ds(start, size))]
                else:
                    source = slots[chain * levels + turn - 1].at[away]
                flying[chain] = pltpu.make_async_remote_copy(
                    src_ref=source,
                    dst_ref=slots[chain * levels + turn],
                    send_sem=send_sems.at[chain, turn],
                    recv_sem=recv_sems.at[chain, turn],
                    device_id=(partners[order[turn]],),
                    device_id_type=pl.DeviceIdType.MESH,
                )
                flying[chain].start()


def scatter_all(blocks, orders):
    levels = len(orders[0])
    rows = blocks[0].shape[0] >> levels
    if rows % 16:
        return [scatter_rows(block, "fsdp", order) for block, order in zip(blocks, orders)]
    count = len(blocks)
    slots = []
    for block in blocks:
        for lane in range(len(orders)):
            size = column_runs(block.shape[1])[lane][1]
            for turn in range(levels):
                slots.append(pltpu.VMEM((2,) * (levels - 1 - turn) + (rows, size), block.dtype))
    chains = count * len(orders)
    return pl.pallas_call(
        functools.partial(scatter_kernel, orders, count),
        out_shape=[jax.ShapeDtypeStruct((rows, block.shape[1]), jnp.float32) for block in blocks],
        in_specs=[pl.BlockSpec(memory_space=pltpu.VMEM)] * count,
        out_specs=[pl.BlockSpec(memory_space=pltpu.VMEM)] * count,
        scratch_shapes=slots
        + [
            pltpu.SemaphoreType.DMA((chains, levels)),
            pltpu.SemaphoreType.DMA((chains, levels)),
        ],
        compiler_params=pltpu.CompilerParams(
            collective_id=3, has_side_effects=True, vmem_limit_bytes=40 << 20
        ),
        name="scatter",
    )(*[block.reshape((2,) * levels + (rows, block.shape[1])) for block in blocks])


def combine_kernel(levels, merge, in_ref, out_ref, slots, send_sems, recv_sems):
    me = lax.axis_index("fsdp")
    partners = []
    for bit in range(levels):
        step = 1 << bit
        partners.append(me + step - 2 * step * ((me // step) % 2))
    barrier = pltpu.get_barrier_semaphore()
    for partner in partners:
        pl.semaphore_signal(
            barrier, inc=1, device_id=(partner,), device_id_type=pl.DeviceIdType.MESH
        )
    pl.semaphore_wait(barrier, levels)
    slots[0] = in_ref[...]
    for bit in range(levels):
        copy = pltpu.make_async_remote_copy(
            src_ref=slots.at[2 * bit],
            dst_ref=slots.at[2 * bit + 1],
            send_sem=send_sems.at[bit],
            recv_sem=recv_sems.at[bit],
            device_id=(partners[bit],),
            device_id_type=pl.DeviceIdType.MESH,
        )
        copy.start()
        copy.wait()
        slots[2 * bit + 2] = merge(slots[2 * bit], slots[2 * bit + 1], 1 << bit)
    out_ref[...] = slots[2 * levels]


def combine(rows, merge, name, collective_id):
    levels = lax.axis_size("fsdp").bit_length() - 1
    return pl.pallas_call(
        functools.partial(combine_kernel, levels, merge),
        out_shape=jax.ShapeDtypeStruct(rows.shape, rows.dtype),
        in_specs=[pl.BlockSpec(memory_space=pltpu.VMEM)],
        out_specs=pl.BlockSpec(memory_space=pltpu.VMEM),
        scratch_shapes=[
            pltpu.VMEM((2 * levels + 1,) + rows.shape, rows.dtype),
            pltpu.SemaphoreType.DMA((levels,)),
            pltpu.SemaphoreType.DMA((levels,)),
        ],
        compiler_params=pltpu.CompilerParams(collective_id=collective_id, has_side_effects=True),
        name=name,
    )(rows)


def merge_sums(left, right, blocks):
    return left + right


def product(left, right):
    return jnp.dot(left, right, preferred_element_type=jnp.float32)


def product_left(left, right):
    return lax.dot_general(
        left, right, (((0,), (0,)), ((), ())), preferred_element_type=jnp.float32
    )


def product_right(left, right):
    return lax.dot_general(
        left, right, (((1,), (1,)), ((), ())), preferred_element_type=jnp.float32
    )


def contract(form, left, right):
    return jnp.einsum(form, left, right, preferred_element_type=jnp.float32)


def norm_forward(inputs, gain, shift):
    mean = jnp.mean(inputs, -1, keepdims=True)
    centred = inputs - mean
    inverse = lax.rsqrt(jnp.mean(centred * centred, -1, keepdims=True) + EPS)
    scaled = centred * inverse
    return (scaled * gain + shift, scaled, inverse)


def norm_backward(grad, scaled, inverse, gain):
    inner = grad * gain
    result = inverse * (
        inner
        - jnp.mean(inner, -1, keepdims=True)
        - scaled * jnp.mean(inner * scaled, -1, keepdims=True)
    )
    return (result, jnp.sum(grad * scaled, 0), jnp.sum(grad, 0))


def swish_slope(hidden):
    sigma = jax.nn.sigmoid(hidden)
    return sigma * (1.0 + hidden * (1.0 - sigma))


def position_table(length, width):
    count = 2 * length - 1
    distance = (length - 1 - jnp.arange(count)).astype(jnp.float32)[:, None]
    freqs = jnp.exp(
        -math.log(10000.0) * (2.0 * jnp.arange(width // 2).astype(jnp.float32)) / width
    )[None, :]
    angles = distance * freqs
    return jnp.concatenate([jnp.sin(angles), jnp.cos(angles)], 1).astype(jnp.bfloat16)


def skew(full):
    lead = full.shape[:-2]
    length = full.shape[-2]
    span = full.shape[-1]
    flat = full.reshape(lead + (length * span,))[..., length - 1 :]
    flat = flat[..., : length * (span - 1)]
    return flat.reshape(lead + (length, span - 1))[..., :length]


def unskew(grad):
    lead = grad.shape[:-2]
    length = grad.shape[-1]
    span = 2 * length - 1
    none = [(0, 0)] * len(lead)
    flat = jnp.pad(grad, none + [(0, 0), (0, span - 1 - length)])
    flat = flat.reshape(lead + (length * (span - 1),))
    flat = jnp.pad(flat, none + [(length - 1, 1)])
    return flat.reshape(lead + (length, span))


def attention_scores(query_u, query_v, keys, relative):
    content = contract("sihe,sjhe->shij", query_u, keys)
    position = contract("sihe,che->shic", query_v, relative)
    return (content + skew(position)) * HEAD ** (-0.5)


def attention_core(query_u, query_v, keys, values, relative):
    scores = attention_scores(query_u, query_v, keys, relative)
    top = jnp.max(scores, -1, keepdims=True)
    logsum = top + jnp.log(jnp.sum(jnp.exp(scores - top), -1, keepdims=True))
    probs = jnp.exp(scores - logsum).astype(jnp.bfloat16)
    context = contract("shij,sjhe->sihe", probs, values)
    return (context.astype(jnp.bfloat16), logsum)


def attention_core_backward(query_u, query_v, keys, values, logsum, grad_context, relative):
    scores = attention_scores(query_u, query_v, keys, relative)
    probs = jnp.exp(scores - logsum)
    probs_low = probs.astype(jnp.bfloat16)
    grad_probs = contract("sihe,sjhe->shij", grad_context, values)
    grad_values = contract("shij,sihe->sjhe", probs_low, grad_context)
    delta = jnp.sum(probs * grad_probs, -1, keepdims=True)
    grad_scores = (probs * (grad_probs - delta) * HEAD ** (-0.5)).astype(jnp.bfloat16)
    grad_u = contract("shij,sjhe->sihe", grad_scores, keys)
    grad_keys = contract("shij,sihe->sjhe", grad_scores, query_u)
    grad_full = unskew(grad_scores)
    grad_v = contract("shic,che->sihe", grad_full, relative)
    grad_relative = contract("shic,sihe->sche", grad_full, query_v).astype(jnp.bfloat16)
    return (grad_u, grad_v, grad_keys, grad_values, grad_relative)


def all_at_once(function, arrays):
    return function(*arrays)


def feed_forward(inputs, gain, shift, weight_up, weight_down):
    normed, scaled, inverse = norm_forward(inputs, gain, shift)
    normed_low = normed.astype(jnp.bfloat16)
    hidden = product(normed_low, weight_up)
    active = (hidden * jax.nn.sigmoid(hidden)).astype(jnp.bfloat16)
    return (
        inputs + 0.5 * product_right(active, weight_down),
        (normed_low, scaled, inverse, hidden, active),
    )


def feed_backward(grad, saved, gain, weight_up, weight_down):
    normed_low, scaled, inverse, hidden, active = saved
    down_low = (0.5 * grad).astype(jnp.bfloat16)
    grad_down = product_left(down_low, active)
    grad_hidden = (product(down_low, weight_down) * swish_slope(hidden)).astype(jnp.bfloat16)
    grad_up = product_left(normed_low, grad_hidden)
    grad_input, grad_gain, grad_shift = norm_backward(
        product_right(grad_hidden, weight_up), scaled, inverse, gain
    )
    return (grad + grad_input, grad_up, grad_down, grad_gain, grad_shift)


def attention_layer(inputs, params, project_in, project_out, table, sequences, runner):
    width = inputs.shape[1]
    length = inputs.shape[0] // sequences
    normed, scaled, inverse = norm_forward(inputs, params[2], params[3])
    normed_low = normed.astype(jnp.bfloat16)
    joint = product(normed_low, project_in[:, : 3 * width])
    query = joint[:, :width]
    shape = (sequences, length, HEADS, width // HEADS)
    keys = joint[:, width : 2 * width].astype(jnp.bfloat16).reshape(shape)
    values = joint[:, 2 * width :].astype(jnp.bfloat16).reshape(shape)
    query_u = (query + params[12]).astype(jnp.bfloat16).reshape(shape)
    query_v = (query + params[13]).astype(jnp.bfloat16).reshape(shape)
    relative = (
        product(table, project_in[:, 3 * width :])
        .astype(jnp.bfloat16)
        .reshape(2 * length - 1, HEADS, width // HEADS)
    )

    def attend(part_u, part_v, part_keys, part_values):
        return attention_core(part_u, part_v, part_keys, part_values, relative)

    context, logsum = runner(attend, (query_u, query_v, keys, values))
    context = context.reshape(-1, width)
    saved = (normed_low, scaled, inverse, query_u, query_v, keys, values, relative, logsum, context)
    return (inputs + product(context, project_out), saved)


def attention_layer_backward(
    grad, saved, params, project_in, project_out, table, sequences, runner
):
    normed_low, scaled, inverse, query_u, query_v, keys, values, relative, logsum, context = saved
    width = grad.shape[1]
    grad_low = grad.astype(jnp.bfloat16)
    grad_out = product_left(context, grad_low)
    grad_context = product_right(grad_low, project_out).astype(jnp.bfloat16).reshape(query_u.shape)

    def attend_back(part_u, part_v, part_keys, part_values, part_logsum, part_grad):
        return attention_core_backward(
            part_u, part_v, part_keys, part_values, part_logsum, part_grad, relative
        )

    grad_u, grad_v, grad_keys, grad_values, grad_relative = runner(
        attend_back, (query_u, query_v, keys, values, logsum, grad_context)
    )
    grad_joint = jnp.concatenate(
        [
            (grad_u + grad_v).reshape(-1, width),
            grad_keys.reshape(-1, width),
            grad_values.reshape(-1, width),
        ],
        1,
    ).astype(jnp.bfloat16)
    grad_joint_in = product_left(normed_low, grad_joint)
    span = relative.shape[0]
    grad_position = product_left(
        jnp.tile(table, (sequences, 1)), grad_relative.reshape(sequences * span, width)
    )
    grad_in = jnp.concatenate([grad_joint_in, grad_position], 1)
    grad_input, grad_gain, grad_shift = norm_backward(
        product_right(grad_joint, project_in[:, : 3 * width]), scaled, inverse, params[2]
    )
    return (
        grad + grad_input,
        grad_in,
        grad_out,
        grad_gain,
        grad_shift,
        jnp.sum(grad_u, (0, 1)).reshape(width),
        jnp.sum(grad_v, (0, 1)).reshape(width),
    )


def mixer_head(inputs, gain, shift, weight_up, taps, sequences):
    normed, scaled, inverse = norm_forward(inputs, gain, shift)
    normed_low = normed.astype(jnp.bfloat16)
    joint = product(normed_low, weight_up)
    width = inputs.shape[1]
    sigma = jax.nn.sigmoid(joint[:, width:])
    gated = joint[:, :width] * sigma
    length = inputs.shape[0] // sequences
    half = (taps.shape[0] - 1) // 2
    padded = jnp.pad(gated.reshape(sequences, length, width), ((0, 0), (half, half), (0, 0)))
    depth = jnp.zeros((sequences, length, width), jnp.float32)
    for offset in range(taps.shape[0]):
        depth = depth + taps[offset] * padded[:, offset : offset + length]
    return (depth.reshape(-1, width), (normed_low, scaled, inverse, joint, sigma, padded))


def mixer_backward(grad, grad_depth, saved, taps, weight_up, gain, sequences):
    normed_low, scaled, inverse, joint, sigma, padded = saved
    width = grad.shape[1]
    length = grad.shape[0] // sequences
    kernel = taps.shape[0]
    half = (kernel - 1) // 2
    grad_cube = grad_depth.reshape(sequences, length, width)
    grad_padded = jnp.pad(grad_cube, ((0, 0), (half, half), (0, 0)))
    grad_gated = jnp.zeros((sequences, length, width), jnp.float32)
    tap_rows = []
    for offset in range(kernel):
        start = kernel - 1 - offset
        grad_gated = grad_gated + taps[offset] * grad_padded[:, start : start + length]
        tap_rows.append(jnp.sum(grad_cube * padded[:, offset : offset + length], (0, 1)))
    grad_gated = grad_gated.reshape(-1, width)
    grad_joint = jnp.concatenate(
        [grad_gated * sigma, grad_gated * joint[:, :width] * sigma * (1.0 - sigma)], 1
    ).astype(jnp.bfloat16)
    grad_up = product_left(normed_low, grad_joint)
    grad_input, grad_gain, grad_shift = norm_backward(
        product_right(grad_joint, weight_up), scaled, inverse, gain
    )
    return (grad + grad_input, grad_up, jnp.stack(tap_rows), grad_gain, grad_shift)


def micro_step(
    rows, incoming, forward_set, backward_set, sequences, batch_stats, grad_stats, runner
):
    (
        project_in,
        project_out,
        first_up,
        first_down,
        second_up,
        second_down,
        mixer_up,
        mixer_taps,
        mixer_down,
        packed,
    ) = forward_set
    params = packed.astype(jnp.float32)
    taps = mixer_taps.astype(jnp.float32)
    table = position_table(SEQ_LEN, rows.shape[1])
    inputs = rows.astype(jnp.float32)
    after_first, saved_first = feed_forward(inputs, params[0], params[1], first_up, first_down)
    after_attention, saved_attention = attention_layer(
        after_first, params, project_in, project_out, table, sequences, runner
    )
    depth, saved_mixer = mixer_head(
        after_attention, params[4], params[5], mixer_up, taps, sequences
    )
    batch_mean, batch_var = batch_stats(depth)
    inverse_var = lax.rsqrt(batch_var + EPS)
    batch_normal = (depth - batch_mean) * inverse_var
    batch_active = batch_normal * params[10] + params[11]
    mixer_active = (batch_active * jax.nn.sigmoid(batch_active)).astype(jnp.bfloat16)
    after_mixer = after_attention + product(mixer_active, mixer_down)
    after_second, saved_second = feed_forward(
        after_mixer, params[6], params[7], second_up, second_down
    )
    final, final_scaled, final_inverse = norm_forward(after_second, params[8], params[9])
    (
        project_in,
        project_out,
        first_up,
        first_down,
        second_up,
        second_down,
        mixer_up,
        mixer_taps,
        mixer_down,
        packed,
    ) = backward_set
    params = packed.astype(jnp.float32)
    taps = mixer_taps.astype(jnp.float32)
    grad_rows = incoming.astype(jnp.float32)
    grad_second, gain_final, shift_final = norm_backward(
        grad_rows, final_scaled, final_inverse, params[8]
    )
    grad_mixer, grad_second_up, grad_second_down, gain_second, shift_second = feed_backward(
        grad_second, saved_second, params[6], second_up, second_down
    )
    early = jnp.concatenate([grad_second_up, grad_second_down], 1).astype(jnp.bfloat16)
    grad_mixer, early = lax.optimization_barrier((grad_mixer, early))
    order = bit_orders(lax.axis_size("fsdp").bit_length() - 1)[0]
    early = scatter_turns(split_rows(early, "fsdp"), "fsdp", order, 0, 3)
    mixer_low = grad_mixer.astype(jnp.bfloat16)
    grad_mixer_down = product_left(mixer_active, mixer_low)
    grad_batch = product_right(mixer_low, mixer_down) * swish_slope(batch_active)
    mean_grad, mean_cross = grad_stats(grad_batch, batch_normal)
    grad_depth = params[10] * inverse_var * (grad_batch - mean_grad - batch_normal * mean_cross)
    grad_attention, grad_mixer_up, grad_taps, gain_mixer, shift_mixer = mixer_backward(
        grad_mixer, grad_depth, saved_mixer, taps, mixer_up, params[4], sequences
    )
    (
        grad_first,
        grad_project_in,
        grad_project_out,
        gain_attention,
        shift_attention,
        grad_bias_u,
        grad_bias_v,
    ) = attention_layer_backward(
        grad_attention, saved_attention, params, project_in, project_out, table, sequences, runner
    )
    grad_first, early = lax.optimization_barrier((grad_first, early))
    early = scatter_turns(early, "fsdp", order, 3, len(order))
    grad_inputs, grad_first_up, grad_first_down, gain_first, shift_first = feed_backward(
        grad_first, saved_first, params[0], first_up, first_down
    )
    grad_packed = jnp.stack(
        [
            gain_first,
            shift_first,
            gain_attention,
            shift_attention,
            gain_mixer,
            shift_mixer,
            gain_second,
            shift_second,
            gain_final,
            shift_final,
            jnp.sum(grad_batch * batch_normal, 0),
            jnp.sum(grad_batch, 0),
            grad_bias_u,
            grad_bias_v,
        ]
    )
    grads = (
        grad_project_in,
        grad_project_out,
        grad_first_up,
        grad_first_down,
        grad_mixer_up,
        grad_taps,
        grad_mixer_down,
        grad_packed,
    )
    return (early, final.astype(jnp.bfloat16), grad_inputs.astype(jnp.bfloat16), grads)


def on_device(
    tokens,
    cotangent,
    attention_in,
    attention_out,
    first_in,
    first_out,
    second_in,
    second_out,
    pointwise_in,
    depthwise,
    pointwise_out,
    vectors,
):
    block = tokens.shape[0] // MICRO
    sequences = block // SEQ_LEN
    owners = lax.axis_size("fsdp")
    count = block * owners

    def merge_moments(left, right, blocks):
        gap = left[0:1] - right[0:1]
        mean = 0.5 * (left[0:1] + right[0:1])
        squares = left[1:2] + right[1:2] + (0.5 * blocks * block) * gap * gap
        return jnp.concatenate([mean, squares], 0)

    def batch_stats(depth):
        mean = jnp.mean(depth, 0, keepdims=True)
        centred = depth - mean
        moments = jnp.concatenate([mean, jnp.sum(centred * centred, 0, keepdims=True)], 0)
        moments = combine(moments, merge_moments, "moments", 0)
        return (moments[0], moments[1] / count)

    def grad_stats(grad_batch, batch_normal):
        sums = jnp.stack([jnp.sum(grad_batch, 0), jnp.sum(grad_batch * batch_normal, 0)])
        sums = combine(sums, merge_sums, "sums", 1)
        return (sums[0] / count, sums[1] / count)

    orders = bit_orders(owners.bit_length() - 1)
    small = jnp.concatenate([depthwise, vectors], 0)
    small = jnp.pad(small.T, ((0, 0), (0, 128 - small.shape[0])))
    first, middle, second = gather_all(
        (
            jnp.concatenate([first_in, first_out.T, small], 1),
            jnp.concatenate([attention_in, attention_out, pointwise_in, pointwise_out], 1),
            jnp.concatenate([second_in, second_out.T], 1),
        ),
        orders,
    )
    width = first_out.shape[0]
    packed = first[:, 2 * width :].T
    taps = depthwise.shape[0]
    cuts = [attention_in.shape[1]]
    for part in (attention_out, pointwise_in):
        cuts.append(cuts[-1] + part.shape[1])
    shared = (
        middle[:, : cuts[0]],
        middle[:, cuts[0] : cuts[1]],
        first[:, :width],
        first[:, width : 2 * width],
        second[:, :width],
        second[:, width:],
        middle[:, cuts[1] : cuts[2]],
        packed[:taps],
        middle[:, cuts[2] :],
        packed[taps : taps + vectors.shape[0]],
    )
    second, result, grad_rows, grads = micro_step(
        tokens, cotangent, shared, shared, sequences, batch_stats, grad_stats, all_at_once
    )
    low = [grad.astype(jnp.bfloat16) for grad in grads]
    small = jnp.concatenate([low[5], low[7]], 0)
    small = jnp.pad(small.T, ((0, 0), (0, 128 - small.shape[0])))
    middle, first = scatter_all(
        (
            jnp.concatenate([low[0], low[1], low[4], low[6]], 1),
            jnp.concatenate([low[2], low[3], small], 1),
        ),
        orders,
    )
    packed = first[:, 2 * width :].T
    return (
        result,
        grad_rows,
        middle[:, : cuts[0]],
        middle[:, cuts[0] : cuts[1]],
        first[:, :width],
        first[:, width : 2 * width].T,
        second[:, :width],
        second[:, width:].T,
        middle[:, cuts[1] : cuts[2]],
        packed[:taps],
        middle[:, cuts[2] :],
        packed[taps : taps + vectors.shape[0]],
    )


def solution(mesh):
    return jax.shard_map(
        on_device,
        mesh=mesh,
        in_specs=(
            P("fsdp", None),
            P("fsdp", None),
            P("fsdp", None),
            P("fsdp", None),
            P("fsdp", None),
            P(None, "fsdp"),
            P("fsdp", None),
            P(None, "fsdp"),
            P("fsdp", None),
            P(None, "fsdp"),
            P("fsdp", None),
            P(None, "fsdp"),
        ),
        out_specs=(
            P("fsdp", None),
            P("fsdp", None),
            P("fsdp", None),
            P("fsdp", None),
            P("fsdp", None),
            P(None, "fsdp"),
            P("fsdp", None),
            P(None, "fsdp"),
            P("fsdp", None),
            P(None, "fsdp"),
            P("fsdp", None),
            P(None, "fsdp"),
        ),
        check_vma=False,
    )
```

```python
import functools
import math

import jax
import jax.numpy as jnp
from jax import lax
from jax.experimental import pallas as pl
from jax.experimental.pallas import tpu as pltpu
from jax.sharding import PartitionSpec as P

HEADS = 8
HEAD = 64
SEQ_LEN = 180
MICRO = 1


EPS = 1e-05


def exchange(block, axis, bit):
    count = lax.axis_size(axis)
    return lax.ppermute(block, axis, [(low, low ^ 1 << bit) for low in range(count)])


def bit_orders(levels):
    rest = list(range(1, levels))
    if levels == 5:
        return ((0, 1, 2, 3, 4), (0, 2, 1, 3, 4), (0, 3, 4, 1, 2))
    third = max(1, len(rest) // 3)
    return tuple(tuple([0] + rest[k:] + rest[:k]) for k in (0, third, 2 * third))


def gather_rows(shard, axis, order):
    me = lax.axis_index(axis)
    current = shard
    have = []
    for bit in reversed(order):
        other = exchange(current, axis, bit)
        have = sorted(have + [bit], reverse=True)
        low = jnp.right_shift(me, bit) % 2 == 0
        current = jnp.stack(
            [jnp.where(low, current, other), jnp.where(low, other, current)], have.index(bit)
        )
    return current.reshape(-1, shard.shape[1])


def scatter_rows(block, axis, order):
    count = lax.axis_size(axis)
    me = lax.axis_index(axis)
    current = block.reshape((2,) * len(order) + (block.shape[0] // count, block.shape[1]))
    left = sorted(order, reverse=True)
    for step, bit in enumerate(order):
        place = left.index(bit)
        left.remove(bit)
        mine = jnp.right_shift(me, bit) % 2
        keep = lax.dynamic_index_in_dim(current, mine, place, False)
        send = lax.dynamic_index_in_dim(current, 1 - mine, place, False)
        current = keep.astype(jnp.float32) + exchange(send, axis, bit).astype(jnp.float32)
        if step + 1 < len(order):
            current = current.astype(jnp.bfloat16)
    return current


def partner_of(me, bit):
    step = 1 << bit
    return me + step - 2 * step * ((me // step) % 2)


def column_runs(width):
    large = width * 7 // 16 // 128 * 128
    return ((0, large), (large, large), (2 * large, width - 2 * large))


def gather_kernel(orders, count, *refs):
    levels = len(orders[0])
    shards = refs[:count]
    wholes = refs[count : 2 * count]
    local_sems, send_sems, recv_sems = refs[2 * count :]
    me = lax.axis_index("fsdp")
    partners = [partner_of(me, bit) for bit in range(levels)]
    barrier = pltpu.get_barrier_semaphore()
    for partner in partners:
        pl.semaphore_signal(
            barrier, inc=1, device_id=(partner,), device_id_type=pl.DeviceIdType.MESH
        )
    pl.semaphore_wait(barrier, levels)

    def held(done):
        return tuple(
            slice(None) if bit in done else (me // (1 << bit)) % 2
            for bit in reversed(range(levels))
        )

    own = []
    for index in range(count):
        own.append(
            pltpu.make_async_copy(
                shards[index], wholes[index].at[held(())], local_sems.at[index]
            )
        )
        own[-1].start()
    flying = {}
    for step in range(levels + count - 1):
        for index in range(count):
            turn = step - index
            if turn < 0 or turn >= levels:
                continue
            width = shards[index].shape[1]
            for lane, order in enumerate(orders):
                start, size = column_runs(width)[lane]
                chain = index * len(orders) + lane
                route = order[::-1]
                if turn > 0:
                    flying[chain].wait()
                    if turn == 1 and lane == 0:
                        own[index].wait()
                columns = pl.ds(start, size)
                slot = wholes[index].at[held(route[:turn]) + (slice(None), columns)]
                source = shards[index].at[:, columns] if turn == 0 else slot
                flying[chain] = pltpu.make_async_remote_copy(
                    src_ref=source,
                    dst_ref=slot,
                    send_sem=send_sems.at[chain, turn],
                    recv_sem=recv_sems.at[chain, turn],
                    device_id=(partners[route[turn]],),
                    device_id_type=pl.DeviceIdType.MESH,
                )
                flying[chain].start()
    for copy in flying.values():
        copy.wait()


def gather_all(shards, orders):
    if shards[0].shape[0] % 16:
        return [gather_rows(shard, "fsdp", order) for shard, order in zip(shards, orders * 2)]
    levels = len(orders[0])
    count = len(shards)
    wholes = pl.pallas_call(
        functools.partial(gather_kernel, orders, count),
        out_shape=[
            jax.ShapeDtypeStruct((2,) * levels + shard.shape, shard.dtype) for shard in shards
        ],
        in_specs=[pl.BlockSpec(memory_space=pl.ANY)] * count,
        out_specs=[pl.BlockSpec(memory_space=pl.ANY)] * count,
        scratch_shapes=[
            pltpu.SemaphoreType.DMA((count,)),
            pltpu.SemaphoreType.DMA((count * len(orders), levels)),
            pltpu.SemaphoreType.DMA((count * len(orders), levels)),
        ],
        compiler_params=pltpu.CompilerParams(collective_id=2, has_side_effects=True),
        name="gather",
    )(*shards)
    return [whole.reshape(-1, whole.shape[-1]) for whole in wholes]


def scatter_kernel(orders, count, *refs):
    levels = len(orders[0])
    grads = refs[:count]
    sums = refs[count : 2 * count]
    chains = count * len(orders)
    slots = refs[2 * count : -2]
    send_sems, recv_sems = refs[-2:]
    me = lax.axis_index("fsdp")
    partners = [partner_of(me, bit) for bit in range(levels)]
    mine = [(me // (1 << bit)) % 2 for bit in range(levels)]
    barrier = pltpu.get_barrier_semaphore()
    for partner in partners:
        pl.semaphore_signal(
            barrier, inc=1, device_id=(partner,), device_id_type=pl.DeviceIdType.MESH
        )
    pl.semaphore_wait(barrier, levels)

    def place_of(order, turn):
        left = sorted(order[turn:], reverse=True)
        return left.index(order[turn])

    def add(index, lane, turn):
        order = orders[lane]
        start, size = column_runs(grads[index].shape[-1])[lane]
        chain = index * len(orders) + lane
        columns = pl.ds(start, size)
        place = place_of(order, turn)
        depth = levels - 1 - turn
        arrived = slots[chain * levels + turn]
        before = slots[chain * levels + turn - 1]

        def body(block, carry):
            where = [(block // (1 << k)) % 2 for k in reversed(range(depth))]
            inner = tuple(where[:place] + [mine[order[turn]]] + where[place:])
            rows = (slice(None), slice(None))
            if turn == 0:
                kept = grads[index][inner + (slice(None), columns)]
            else:
                kept = before[inner + rows]
            total = kept.astype(jnp.float32) + arrived[tuple(where) + rows].astype(jnp.float32)
            if depth == 0:
                sums[index][:, columns] = total
            else:
                arrived[tuple(where) + rows] = total.astype(arrived.dtype)
            return carry

        if depth == 0:
            body(0, 0)
        else:
            lax.fori_loop(0, 1 << depth, body, 0)

    flying = {}
    for step in range(levels + count):
        for index in range(count):
            turn = step - index
            if turn < 0 or turn > levels:
                continue
            for lane, order in enumerate(orders):
                start, size = column_runs(grads[index].shape[-1])[lane]
                chain = index * len(orders) + lane
                if turn > 0:
                    flying[chain].wait()
                    add(index, lane, turn - 1)
                if turn == levels:
                    continue
                place = place_of(order, turn)
                away = (slice(None),) * place + (1 - mine[order[turn]],)
                away = away + (slice(None),) * (levels - 1 - turn - place)
                if turn == 0:
                    source = grads[index].at[away + (slice(None), pl.ds(start, size))]
                else:
                    source = slots[chain * levels + turn - 1].at[away]
                flying[chain] = pltpu.make_async_remote_copy(
                    src_ref=source,
                    dst_ref=slots[chain * levels + turn],
                    send_sem=send_sems.at[chain, turn],
                    recv_sem=recv_sems.at[chain, turn],
                    device_id=(partners[order[turn]],),
                    device_id_type=pl.DeviceIdType.MESH,
                )
                flying[chain].start()


def scatter_all(blocks, orders):
    levels = len(orders[0])
    rows = blocks[0].shape[0] >> levels
    if rows % 16:
        return [scatter_rows(block, "fsdp", order) for block, order in zip(blocks, orders)]
    count = len(blocks)
    slots = []
    for block in blocks:
        for lane in range(len(orders)):
            size = column_runs(block.shape[1])[lane][1]
            for turn in range(levels):
                slots.append(pltpu.VMEM((2,) * (levels - 1 - turn) + (rows, size), block.dtype))
    chains = count * len(orders)
    return pl.pallas_call(
        functools.partial(scatter_kernel, orders, count),
        out_shape=[jax.ShapeDtypeStruct((rows, block.shape[1]), jnp.float32) for block in blocks],
        in_specs=[pl.BlockSpec(memory_space=pltpu.VMEM)] * count,
        out_specs=[pl.BlockSpec(memory_space=pltpu.VMEM)] * count,
        scratch_shapes=slots
        + [
            pltpu.SemaphoreType.DMA((chains, levels)),
            pltpu.SemaphoreType.DMA((chains, levels)),
        ],
        compiler_params=pltpu.CompilerParams(
            collective_id=3, has_side_effects=True, vmem_limit_bytes=40 << 20
        ),
        name="scatter",
    )(*[block.reshape((2,) * levels + (rows, block.shape[1])) for block in blocks])


def combine_kernel(levels, merge, in_ref, out_ref, slots, send_sems, recv_sems):
    me = lax.axis_index("fsdp")
    partners = []
    for bit in range(levels):
        step = 1 << bit
        partners.append(me + step - 2 * step * ((me // step) % 2))
    barrier = pltpu.get_barrier_semaphore()
    for partner in partners:
        pl.semaphore_signal(
            barrier, inc=1, device_id=(partner,), device_id_type=pl.DeviceIdType.MESH
        )
    pl.semaphore_wait(barrier, levels)
    slots[0] = in_ref[...]
    for bit in range(levels):
        copy = pltpu.make_async_remote_copy(
            src_ref=slots.at[2 * bit],
            dst_ref=slots.at[2 * bit + 1],
            send_sem=send_sems.at[bit],
            recv_sem=recv_sems.at[bit],
            device_id=(partners[bit],),
            device_id_type=pl.DeviceIdType.MESH,
        )
        copy.start()
        copy.wait()
        slots[2 * bit + 2] = merge(slots[2 * bit], slots[2 * bit + 1], 1 << bit)
    out_ref[...] = slots[2 * levels]


def combine(rows, merge, name, collective_id):
    levels = lax.axis_size("fsdp").bit_length() - 1
    return pl.pallas_call(
        functools.partial(combine_kernel, levels, merge),
        out_shape=jax.ShapeDtypeStruct(rows.shape, rows.dtype),
        in_specs=[pl.BlockSpec(memory_space=pltpu.VMEM)],
        out_specs=pl.BlockSpec(memory_space=pltpu.VMEM),
        scratch_shapes=[
            pltpu.VMEM((2 * levels + 1,) + rows.shape, rows.dtype),
            pltpu.SemaphoreType.DMA((levels,)),
            pltpu.SemaphoreType.DMA((levels,)),
        ],
        compiler_params=pltpu.CompilerParams(collective_id=collective_id, has_side_effects=True),
        name=name,
    )(rows)


def merge_sums(left, right, blocks):
    return left + right


def product(left, right):
    return jnp.dot(left, right, preferred_element_type=jnp.float32)


def product_left(left, right):
    return lax.dot_general(
        left, right, (((0,), (0,)), ((), ())), preferred_element_type=jnp.float32
    )


def product_right(left, right):
    return lax.dot_general(
        left, right, (((1,), (1,)), ((), ())), preferred_element_type=jnp.float32
    )


def contract(form, left, right):
    return jnp.einsum(form, left, right, preferred_element_type=jnp.float32)


def norm_forward(inputs, gain, shift):
    mean = jnp.mean(inputs, -1, keepdims=True)
    centred = inputs - mean
    inverse = lax.rsqrt(jnp.mean(centred * centred, -1, keepdims=True) + EPS)
    scaled = centred * inverse
    return (scaled * gain + shift, scaled, inverse)


def norm_backward(grad, scaled, inverse, gain):
    inner = grad * gain
    result = inverse * (
        inner
        - jnp.mean(inner, -1, keepdims=True)
        - scaled * jnp.mean(inner * scaled, -1, keepdims=True)
    )
    return (result, jnp.sum(grad * scaled, 0), jnp.sum(grad, 0))


def swish_slope(hidden):
    sigma = jax.nn.sigmoid(hidden)
    return sigma * (1.0 + hidden * (1.0 - sigma))


def position_table(length, width):
    count = 2 * length - 1
    distance = (length - 1 - jnp.arange(count)).astype(jnp.float32)[:, None]
    freqs = jnp.exp(
        -math.log(10000.0) * (2.0 * jnp.arange(width // 2).astype(jnp.float32)) / width
    )[None, :]
    angles = distance * freqs
    return jnp.concatenate([jnp.sin(angles), jnp.cos(angles)], 1).astype(jnp.bfloat16)


def skew(full):
    lead = full.shape[:-2]
    length = full.shape[-2]
    span = full.shape[-1]
    flat = full.reshape(lead + (length * span,))[..., length - 1 :]
    flat = flat[..., : length * (span - 1)]
    return flat.reshape(lead + (length, span - 1))[..., :length]


def unskew(grad):
    lead = grad.shape[:-2]
    length = grad.shape[-1]
    span = 2 * length - 1
    none = [(0, 0)] * len(lead)
    flat = jnp.pad(grad, none + [(0, 0), (0, span - 1 - length)])
    flat = flat.reshape(lead + (length * (span - 1),))
    flat = jnp.pad(flat, none + [(length - 1, 1)])
    return flat.reshape(lead + (length, span))


def attention_scores(query_u, query_v, keys, relative):
    content = contract("sihe,sjhe->shij", query_u, keys)
    position = contract("sihe,che->shic", query_v, relative)
    return (content + skew(position)) * HEAD ** (-0.5)


def attention_core(query_u, query_v, keys, values, relative):
    scores = attention_scores(query_u, query_v, keys, relative)
    top = jnp.max(scores, -1, keepdims=True)
    logsum = top + jnp.log(jnp.sum(jnp.exp(scores - top), -1, keepdims=True))
    probs = jnp.exp(scores - logsum).astype(jnp.bfloat16)
    context = contract("shij,sjhe->sihe", probs, values)
    return (context.astype(jnp.bfloat16), logsum)


def attention_core_backward(query_u, query_v, keys, values, logsum, grad_context, relative):
    scores = attention_scores(query_u, query_v, keys, relative)
    probs = jnp.exp(scores - logsum)
    probs_low = probs.astype(jnp.bfloat16)
    grad_probs = contract("sihe,sjhe->shij", grad_context, values)
    grad_values = contract("shij,sihe->sjhe", probs_low, grad_context)
    delta = jnp.sum(probs * grad_probs, -1, keepdims=True)
    grad_scores = (probs * (grad_probs - delta) * HEAD ** (-0.5)).astype(jnp.bfloat16)
    grad_u = contract("shij,sjhe->sihe", grad_scores, keys)
    grad_keys = contract("shij,sihe->sjhe", grad_scores, query_u)
    grad_full = unskew(grad_scores)
    grad_v = contract("shic,che->sihe", grad_full, relative)
    grad_relative = contract("shic,sihe->sche", grad_full, query_v).astype(jnp.bfloat16)
    return (grad_u, grad_v, grad_keys, grad_values, grad_relative)


def all_at_once(function, arrays):
    return function(*arrays)


def feed_forward(inputs, gain, shift, weight_up, weight_down):
    normed, scaled, inverse = norm_forward(inputs, gain, shift)
    normed_low = normed.astype(jnp.bfloat16)
    hidden = product(normed_low, weight_up)
    active = (hidden * jax.nn.sigmoid(hidden)).astype(jnp.bfloat16)
    return (
        inputs + 0.5 * product_right(active, weight_down),
        (normed_low, scaled, inverse, hidden, active),
    )


def feed_backward(grad, saved, gain, weight_up, weight_down):
    normed_low, scaled, inverse, hidden, active = saved
    down_low = (0.5 * grad).astype(jnp.bfloat16)
    grad_down = product_left(down_low, active)
    grad_hidden = (product(down_low, weight_down) * swish_slope(hidden)).astype(jnp.bfloat16)
    grad_up = product_left(normed_low, grad_hidden)
    grad_input, grad_gain, grad_shift = norm_backward(
        product_right(grad_hidden, weight_up), scaled, inverse, gain
    )
    return (grad + grad_input, grad_up, grad_down, grad_gain, grad_shift)


def attention_layer(inputs, params, project_in, project_out, table, sequences, runner):
    width = inputs.shape[1]
    length = inputs.shape[0] // sequences
    normed, scaled, inverse = norm_forward(inputs, params[2], params[3])
    normed_low = normed.astype(jnp.bfloat16)
    joint = product(normed_low, project_in[:, : 3 * width])
    query = joint[:, :width]
    shape = (sequences, length, HEADS, width // HEADS)
    keys = joint[:, width : 2 * width].astype(jnp.bfloat16).reshape(shape)
    values = joint[:, 2 * width :].astype(jnp.bfloat16).reshape(shape)
    query_u = (query + params[12]).astype(jnp.bfloat16).reshape(shape)
    query_v = (query + params[13]).astype(jnp.bfloat16).reshape(shape)
    relative = (
        product(table, project_in[:, 3 * width :])
        .astype(jnp.bfloat16)
        .reshape(2 * length - 1, HEADS, width // HEADS)
    )

    def attend(part_u, part_v, part_keys, part_values):
        return attention_core(part_u, part_v, part_keys, part_values, relative)

    context, logsum = runner(attend, (query_u, query_v, keys, values))
    context = context.reshape(-1, width)
    saved = (normed_low, scaled, inverse, query_u, query_v, keys, values, relative, logsum, context)
    return (inputs + product(context, project_out), saved)


def attention_layer_backward(
    grad, saved, params, project_in, project_out, table, sequences, runner
):
    normed_low, scaled, inverse, query_u, query_v, keys, values, relative, logsum, context = saved
    width = grad.shape[1]
    grad_low = grad.astype(jnp.bfloat16)
    grad_out = product_left(context, grad_low)
    grad_context = product_right(grad_low, project_out).astype(jnp.bfloat16).reshape(query_u.shape)

    def attend_back(part_u, part_v, part_keys, part_values, part_logsum, part_grad):
        return attention_core_backward(
            part_u, part_v, part_keys, part_values, part_logsum, part_grad, relative
        )

    grad_u, grad_v, grad_keys, grad_values, grad_relative = runner(
        attend_back, (query_u, query_v, keys, values, logsum, grad_context)
    )
    grad_joint = jnp.concatenate(
        [
            (grad_u + grad_v).reshape(-1, width),
            grad_keys.reshape(-1, width),
            grad_values.reshape(-1, width),
        ],
        1,
    ).astype(jnp.bfloat16)
    grad_joint_in = product_left(normed_low, grad_joint)
    span = relative.shape[0]
    grad_position = product_left(
        jnp.tile(table, (sequences, 1)), grad_relative.reshape(sequences * span, width)
    )
    grad_in = jnp.concatenate([grad_joint_in, grad_position], 1)
    grad_input, grad_gain, grad_shift = norm_backward(
        product_right(grad_joint, project_in[:, : 3 * width]), scaled, inverse, params[2]
    )
    return (
        grad + grad_input,
        grad_in,
        grad_out,
        grad_gain,
        grad_shift,
        jnp.sum(grad_u, (0, 1)).reshape(width),
        jnp.sum(grad_v, (0, 1)).reshape(width),
    )


def mixer_head(inputs, gain, shift, weight_up, taps, sequences):
    normed, scaled, inverse = norm_forward(inputs, gain, shift)
    normed_low = normed.astype(jnp.bfloat16)
    joint = product(normed_low, weight_up)
    width = inputs.shape[1]
    sigma = jax.nn.sigmoid(joint[:, width:])
    gated = joint[:, :width] * sigma
    length = inputs.shape[0] // sequences
    half = (taps.shape[0] - 1) // 2
    padded = jnp.pad(gated.reshape(sequences, length, width), ((0, 0), (half, half), (0, 0)))
    depth = jnp.zeros((sequences, length, width), jnp.float32)
    for offset in range(taps.shape[0]):
        depth = depth + taps[offset] * padded[:, offset : offset + length]
    return (depth.reshape(-1, width), (normed_low, scaled, inverse, joint, sigma, padded))


def mixer_backward(grad, grad_depth, saved, taps, weight_up, gain, sequences):
    normed_low, scaled, inverse, joint, sigma, padded = saved
    width = grad.shape[1]
    length = grad.shape[0] // sequences
    kernel = taps.shape[0]
    half = (kernel - 1) // 2
    grad_cube = grad_depth.reshape(sequences, length, width)
    grad_padded = jnp.pad(grad_cube, ((0, 0), (half, half), (0, 0)))
    grad_gated = jnp.zeros((sequences, length, width), jnp.float32)
    tap_rows = []
    for offset in range(kernel):
        start = kernel - 1 - offset
        grad_gated = grad_gated + taps[offset] * grad_padded[:, start : start + length]
        tap_rows.append(jnp.sum(grad_cube * padded[:, offset : offset + length], (0, 1)))
    grad_gated = grad_gated.reshape(-1, width)
    grad_joint = jnp.concatenate(
        [grad_gated * sigma, grad_gated * joint[:, :width] * sigma * (1.0 - sigma)], 1
    ).astype(jnp.bfloat16)
    grad_up = product_left(normed_low, grad_joint)
    grad_input, grad_gain, grad_shift = norm_backward(
        product_right(grad_joint, weight_up), scaled, inverse, gain
    )
    return (grad + grad_input, grad_up, jnp.stack(tap_rows), grad_gain, grad_shift)


def micro_step(
    rows, incoming, forward_set, backward_set, sequences, batch_stats, grad_stats, runner
):
    (
        project_in,
        project_out,
        first_up,
        first_down,
        second_up,
        second_down,
        mixer_up,
        mixer_taps,
        mixer_down,
        packed,
    ) = forward_set
    params = packed.astype(jnp.float32)
    taps = mixer_taps.astype(jnp.float32)
    table = position_table(SEQ_LEN, rows.shape[1])
    inputs = rows.astype(jnp.float32)
    after_first, saved_first = feed_forward(inputs, params[0], params[1], first_up, first_down)
    after_attention, saved_attention = attention_layer(
        after_first, params, project_in, project_out, table, sequences, runner
    )
    depth, saved_mixer = mixer_head(
        after_attention, params[4], params[5], mixer_up, taps, sequences
    )
    batch_mean, batch_var = batch_stats(depth)
    inverse_var = lax.rsqrt(batch_var + EPS)
    batch_normal = (depth - batch_mean) * inverse_var
    batch_active = batch_normal * params[10] + params[11]
    mixer_active = (batch_active * jax.nn.sigmoid(batch_active)).astype(jnp.bfloat16)
    after_mixer = after_attention + product(mixer_active, mixer_down)
    after_second, saved_second = feed_forward(
        after_mixer, params[6], params[7], second_up, second_down
    )
    final, final_scaled, final_inverse = norm_forward(after_second, params[8], params[9])
    (
        project_in,
        project_out,
        first_up,
        first_down,
        second_up,
        second_down,
        mixer_up,
        mixer_taps,
        mixer_down,
        packed,
    ) = backward_set
    params = packed.astype(jnp.float32)
    taps = mixer_taps.astype(jnp.float32)
    grad_rows = incoming.astype(jnp.float32)
    grad_second, gain_final, shift_final = norm_backward(
        grad_rows, final_scaled, final_inverse, params[8]
    )
    grad_mixer, grad_second_up, grad_second_down, gain_second, shift_second = feed_backward(
        grad_second, saved_second, params[6], second_up, second_down
    )
    early = jnp.concatenate([grad_second_up, grad_second_down], 1).astype(jnp.bfloat16)
    mixer_low = grad_mixer.astype(jnp.bfloat16)
    grad_mixer_down = product_left(mixer_active, mixer_low)
    grad_batch = product_right(mixer_low, mixer_down) * swish_slope(batch_active)
    mean_grad, mean_cross = grad_stats(grad_batch, batch_normal)
    grad_depth = params[10] * inverse_var * (grad_batch - mean_grad - batch_normal * mean_cross)
    grad_attention, grad_mixer_up, grad_taps, gain_mixer, shift_mixer = mixer_backward(
        grad_mixer, grad_depth, saved_mixer, taps, mixer_up, params[4], sequences
    )
    (
        grad_first,
        grad_project_in,
        grad_project_out,
        gain_attention,
        shift_attention,
        grad_bias_u,
        grad_bias_v,
    ) = attention_layer_backward(
        grad_attention, saved_attention, params, project_in, project_out, table, sequences, runner
    )
    grad_inputs, grad_first_up, grad_first_down, gain_first, shift_first = feed_backward(
        grad_first, saved_first, params[0], first_up, first_down
    )
    grad_packed = jnp.stack(
        [
            gain_first,
            shift_first,
            gain_attention,
            shift_attention,
            gain_mixer,
            shift_mixer,
            gain_second,
            shift_second,
            gain_final,
            shift_final,
            jnp.sum(grad_batch * batch_normal, 0),
            jnp.sum(grad_batch, 0),
            grad_bias_u,
            grad_bias_v,
        ]
    )
    grads = (
        grad_project_in,
        grad_project_out,
        grad_first_up,
        grad_first_down,
        grad_mixer_up,
        grad_taps,
        grad_mixer_down,
        grad_packed,
    )
    return (early, final.astype(jnp.bfloat16), grad_inputs.astype(jnp.bfloat16), grads)


def on_device(
    tokens,
    cotangent,
    attention_in,
    attention_out,
    first_in,
    first_out,
    second_in,
    second_out,
    pointwise_in,
    depthwise,
    pointwise_out,
    vectors,
):
    block = tokens.shape[0] // MICRO
    sequences = block // SEQ_LEN
    owners = lax.axis_size("fsdp")
    count = block * owners

    def merge_moments(left, right, blocks):
        gap = left[0:1] - right[0:1]
        mean = 0.5 * (left[0:1] + right[0:1])
        squares = left[1:2] + right[1:2] + (0.5 * blocks * block) * gap * gap
        return jnp.concatenate([mean, squares], 0)

    def batch_stats(depth):
        mean = jnp.mean(depth, 0, keepdims=True)
        centred = depth - mean
        moments = jnp.concatenate([mean, jnp.sum(centred * centred, 0, keepdims=True)], 0)
        moments = combine(moments, merge_moments, "moments", 0)
        return (moments[0], moments[1] / count)

    def grad_stats(grad_batch, batch_normal):
        sums = jnp.stack([jnp.sum(grad_batch, 0), jnp.sum(grad_batch * batch_normal, 0)])
        sums = combine(sums, merge_sums, "sums", 1)
        return (sums[0] / count, sums[1] / count)

    orders = bit_orders(owners.bit_length() - 1)
    small = jnp.concatenate([depthwise, vectors], 0)
    small = jnp.pad(small.T, ((0, 0), (0, 128 - small.shape[0])))
    first_up, first_down, project, middle, second_up, second_down = gather_all(
        (
            first_in,
            jnp.concatenate([first_out.T, small], 1),
            attention_in,
            jnp.concatenate([attention_out, pointwise_in, pointwise_out], 1),
            second_in,
            second_out.T,
        ),
        orders,
    )
    width = first_out.shape[0]
    packed = first_down[:, width:].T
    taps = depthwise.shape[0]
    cuts = [attention_in.shape[1]]
    for part in (attention_out, pointwise_in):
        cuts.append(cuts[-1] + part.shape[1])
    near, far = attention_out.shape[1], attention_out.shape[1] + pointwise_in.shape[1]
    shared = (
        project,
        middle[:, :near],
        first_up,
        first_down[:, :width],
        second_up,
        second_down,
        middle[:, near:far],
        packed[:taps],
        middle[:, far:],
        packed[taps : taps + vectors.shape[0]],
    )
    second, result, grad_rows, grads = micro_step(
        tokens, cotangent, shared, shared, sequences, batch_stats, grad_stats, all_at_once
    )
    low = [grad.astype(jnp.bfloat16) for grad in grads]
    small = jnp.concatenate([low[5], low[7]], 0)
    small = jnp.pad(small.T, ((0, 0), (0, 128 - small.shape[0])))
    second, middle, first = scatter_all(
        (
            second,
            jnp.concatenate([low[0], low[1], low[4], low[6]], 1),
            jnp.concatenate([low[2], low[3], small], 1),
        ),
        orders,
    )
    packed = first[:, 2 * width :].T
    return (
        result,
        grad_rows,
        middle[:, : cuts[0]],
        middle[:, cuts[0] : cuts[1]],
        first[:, :width],
        first[:, width : 2 * width].T,
        second[:, :width],
        second[:, width:].T,
        middle[:, cuts[1] : cuts[2]],
        packed[:taps],
        middle[:, cuts[2] :],
        packed[taps : taps + vectors.shape[0]],
    )


def solution(mesh):
    return jax.shard_map(
        on_device,
        mesh=mesh,
        in_specs=(
            P("fsdp", None),
            P("fsdp", None),
            P("fsdp", None),
            P("fsdp", None),
            P("fsdp", None),
            P(None, "fsdp"),
            P("fsdp", None),
            P(None, "fsdp"),
            P("fsdp", None),
            P(None, "fsdp"),
            P("fsdp", None),
            P(None, "fsdp"),
        ),
        out_specs=(
            P("fsdp", None),
            P("fsdp", None),
            P("fsdp", None),
            P("fsdp", None),
            P("fsdp", None),
            P(None, "fsdp"),
            P("fsdp", None),
            P(None, "fsdp"),
            P("fsdp", None),
            P(None, "fsdp"),
            P("fsdp", None),
            P(None, "fsdp"),
        ),
        check_vma=False,
    )
```
